32 devices in a mesh: gx: 4 (over y, x), gy: 2 (over core), gz: 4 (over z).
Axes of the slice: x: 2, y: 2, z: 4, core: 2. Of those that a mesh axis runs over, the one named last changes fastest.
Arguments:
- field: bfloat16 [16, 64, 32, 512], P(None, 'gz', 'gy', 'gx'), may hold values from -6 to 6
- fine_taps: float32 [3, 9], replicated, may hold values from 0.1 to 0.6
- coarse_taps: float32 [3, 9], replicated, may hold values from 0.1 to 0.6
- top_kernel: bfloat16 [8, 4, 64, 2048], P('gz', 'gy', 'gx'), may hold values from -6 to 6
Outputs:
- applied: bfloat16 [16, 64, 32, 512], P(None, 'gz', 'gy', 'gx')
The draws below stay inside these ranges and needn't reach their ends.
All inputs are finite; a program needn't handle non-finite values.
Results may differ from the reference program's by a relative error of at most 0.0047.
Values may be sent and summed in bfloat16 or wider, within the bound.
No kernel may reach another device: no remote copies, remote signals or barrier semaphores. Data moves between devices by JAX's collectives and lax.ppermute only.
A program may use at most 128 MiB of HBM per device.

```python
import jax
import jax.numpy as jnp
from jax import lax

V = 16
NX = 512
NY = 32
NZ = 64
TOP = 2048


def level_of(stream_key, extent, pieces, least, top_value):
    level, own = 1.0, jax.random.fold_in(stream_key, 6)
    for position, parts in pieces:
        steps = jnp.exp(jax.random.uniform(jax.random.fold_in(own, position), (parts,), jnp.float32, least / len(pieces), top_value / len(pieces)))
        level = level * jnp.repeat(steps, extent[position] // parts).reshape([-1 if axis == position else 1 for axis in range(len(extent))])
    return level


def noise(rng, extent, width, bound, split=(), dtype=jnp.bfloat16):
    factor_of = level_of(rng, extent, split, -0.22, 0.18) if split else 1.0
    result = jax.random.normal(rng, extent, jnp.float32) * width * factor_of
    return jnp.minimum(jnp.maximum(result, -bound), bound).astype(dtype)


def setup_inputs(seed: int = 0) -> dict:
    splits = jax.random.split(jax.random.key(seed), 5)
    field = noise(splits[0], (V, NZ, NY, NX), 1.0, 6.0, ((1, 4), (2, 2), (3, 4)))
    fine_taps = jnp.clip(jax.random.uniform(splits[1], (3, 9), jnp.float32, 0.1, 0.6), 0.1, 0.6)
    coarse_taps = jnp.clip(jax.random.uniform(splits[2], (3, 9), jnp.float32, 0.1, 0.6), 0.1, 0.6)
    top_kernel = noise(splits[3], (NZ // 8, NY // 8, NX // 8, TOP), (32.0 / TOP ** 0.5), 6.0, ((0, 4), (1, 2), (2, 4)))
    return dict(field=field, fine_taps=fine_taps, coarse_taps=coarse_taps, top_kernel=top_kernel)


def conv_axis(values, kernel_row, along):
    length = values.shape[along]
    widths = [(0, 0)] * values.ndim
    widths[along] = (4, 4)
    padded = jnp.pad(values, widths)
    total = kernel_row[0] * lax.slice_in_dim(padded, 0, length, axis=along)
    for offset in range(1, 9):
        total = total + kernel_row[offset] * lax.slice_in_dim(padded, offset, offset + length, axis=along)
    return total


def separable(values, kernel):
    values = conv_axis(values, kernel[2], 2)
    values = conv_axis(values, kernel[1], 1)
    return conv_axis(values, kernel[0], 0)


def restrict(values, factor):
    depth, rows, cols = values.shape
    return values.reshape(depth // factor, factor, rows // factor, factor, cols // factor, factor).mean(axis=(1, 3, 5))


def prolong(values, factor):
    values = jnp.repeat(values, factor, axis=0)
    values = jnp.repeat(values, factor, axis=1)
    return jnp.repeat(values, factor, axis=2)


def reference(field, fine_taps, coarse_taps, top_kernel):
    def top_input(cells):
        coarse_cells = restrict(cells.astype(jnp.float32), 2)
        return restrict(coarse_cells, 4).astype(jnp.bfloat16)

    top_in = lax.map(top_input, field)
    kernel_rows = top_kernel.reshape(-1, top_kernel.shape[3])
    flat_in = top_in.reshape(top_in.shape[0], -1)
    top_part = lax.dot_general(flat_in, kernel_rows, (((1,), (1,)), ((), ())), preferred_element_type=jnp.float32).reshape(top_in.shape)

    def apply_one(inputs_pair):
        cells, top_piece = inputs_pair
        cells = cells.astype(jnp.float32)
        fine_part = separable(cells, fine_taps)
        coarse_cells = restrict(cells, 2)
        coarse_total = separable(coarse_cells, coarse_taps) + prolong(top_piece, 4)
        return (fine_part + prolong(coarse_total, 2)).astype(jnp.bfloat16)

    return lax.map(apply_one, (field, top_part))
```

```python
import jax
import jax.numpy as jnp
from jax import lax
from jax.experimental import pallas as pl
from jax.experimental.pallas import tpu as pltpu
from jax.sharding import PartitionSpec as P

F32 = jnp.float32
BF16 = jnp.bfloat16
R = 4
E = 2 * R


def swaps(count, kind):
    pairs = []
    for i in range(kind, count - 1, 2):
        pairs += [(i, i + 1), (i + 1, i)]
    return pairs


def kinds(count):
    return [k for k in (0, 1) if swaps(count, k)]


def upper(index, kind):
    return lax.rem(index + kind, 2) == 0


def iota(shape, dim):
    return lax.broadcasted_iota(jnp.int32, shape, dim)


def dot(a, b, dims=((1,), (0,)), precision=None):
    return lax.dot_general(a, b, (dims, ((), ())), precision=precision, preferred_element_type=F32)


def lookup(offset, taps, row):
    total = jnp.zeros(offset.shape, F32)
    for k in range(2 * R + 1):
        total = jnp.where(offset == k, taps[row, k], total)
    return total


def one(condition, value=1.0):
    return jnp.where(condition, value, 0.0).astype(BF16)


def wide(parts):
    return jnp.concatenate(parts, axis=1)


class Sizes:
    def __init__(self, shape, top_shape, mesh_sizes):
        self.V, self.Z, self.Y, self.X = shape
        self.nx, self.ny, self.nz = mesh_sizes
        self.rows = self.Z * self.Y
        self.lanes = self.V * self.X
        self.raw = R * self.Y
        self.avg = (R // 2) * (self.Y // 2)
        self.face = self.raw + self.avg
        self.kx, self.ky, self.kz = kinds(self.nx), kinds(self.ny), kinds(self.nz)
        self.yf, self.yc = self.Z * R, (self.Z // 2) * R
        self.zyf, self.zyc = R * R, R * R
        self.ypack = self.yf + self.yc + len(self.kz) * (self.zyf + self.zyc)
        self.tz, self.ty, self.tx = top_shape
        self.top = self.tz * self.ty * self.tx
        self.gz = self.raw + self.face
        self.tile = self.ty * self.tx * self.nx


def call(body, outs, cost=0, bytes_=0):
    return pl.pallas_call(
        body,
        out_shape=outs,
        cost_estimate=pl.CostEstimate(flops=cost, bytes_accessed=bytes_, transcendentals=0),
    )


def smem():
    return pl.BlockSpec(memory_space=pltpu.SMEM)


def vmem():
    return pl.BlockSpec(memory_space=pltpu.VMEM)


def faces_kernel(s, field, *outs):
    me = lax.axis_index("gz")
    row = iota((s.avg, s.raw), 0)
    col = iota((s.avg, s.raw), 1)
    half = s.Y // 2
    mean = one((col // s.Y // 2 == row // half) & (col % s.Y // 2 == row % half), 0.25)
    for kind, out in zip(s.kz, outs):
        up = upper(me, kind)
        start = jnp.where(up, s.Z - R, 0)
        further = jnp.where(up, s.Z - E, R)
        for v in range(s.V):
            out[v, : s.raw, :] = field[v, pl.ds(start, R)].reshape(s.raw, s.X)
        data = wide([field[v, pl.ds(further, R)].reshape(s.raw, s.X) for v in range(s.V)])
        means = dot(mean, data).astype(BF16)
        for v in range(s.V):
            out[v, s.raw :, :] = means[:, v * s.X : (v + 1) * s.X]


def edges_kernel(s, field, *outs):
    gx = lax.axis_index("gx")
    *edges, piece = outs
    data = wide([field[v].reshape(s.rows, s.X) for v in range(s.V)])
    row = iota((s.lanes, s.V * E), 0)
    lane = iota((s.lanes, s.V * E), 1)
    half = s.Y // 2
    for kind, out in zip(s.kx, edges):
        first = jnp.where(upper(gx, kind), s.X - E, 0)
        pick = one((row // s.X == lane // E) & (row % s.X - first == lane % E))
        packed = dot(data, pick).astype(BF16)
        out[: s.rows, :] = packed
        r = iota((2 * s.avg, s.rows), 0)
        c = iota((2 * s.avg, s.rows), 1)
        layer = r // half * 2 + jnp.where(r < s.avg, R, s.Z - E - R)
        mean = one((c // s.Y // 2 * 2 == layer) & (c % s.Y // 2 == r % half), 0.25)
        out[s.rows :, :] = dot(mean, packed).astype(BF16)
    deep, tall, long = s.Z // s.tz, s.Y // s.ty, s.X // s.tx
    r = iota((8, s.rows), 0)
    c = iota((8, s.rows), 1)
    pool = one(c // s.Y // deep * s.ty + c % s.Y // tall == r, 1.0 / (deep * tall))
    sums = dot(pool, data)
    sub = iota((s.V, s.X), 0)
    x = iota((s.X, s.tile), 0)
    lane = iota((s.X, s.tile), 1)
    for i in range(s.tz):
        total = jnp.zeros((s.V, s.tile), F32)
        for j in range(s.ty):
            p = i * s.ty + j
            by_vector = jnp.zeros((s.V, s.X), F32)
            for v in range(s.V):
                line = jnp.broadcast_to(sums[p : p + 1, v * s.X : (v + 1) * s.X], (s.V, s.X))
                by_vector = jnp.where(sub == v, line, by_vector)
            spread = jnp.where(lane == (j * s.nx + gx) * s.tx + x // long, 1.0 / long, 0.0)
            total = total + dot(by_vector, spread, precision=lax.Precision.HIGHEST)
        piece[i * s.V : (i + 1) * s.V, :] = total.astype(BF16)


def corners_kernel(s, *refs):
    me = lax.axis_index("gz")
    halos, outs = refs[: len(s.kx)], refs[len(s.kx) :]
    for kind, out in zip(s.kz, outs):
        up = upper(me, kind)
        start = pl.multiple_of(jnp.where(up, s.rows - s.raw, 0), 16)
        mean = pl.multiple_of(jnp.where(up, s.rows + s.avg, s.rows), 16)
        for i, halo in enumerate(halos):
            out[i * s.face : i * s.face + s.raw, :] = halo[pl.ds(start, s.raw), :]
            out[i * s.face + s.raw : (i + 1) * s.face, :] = halo[pl.ds(mean, s.avg), :]


def x_weights(s, fine, coarse):
    gx = lax.axis_index("gx")
    blocks = []

    def block(place, count):
        col = iota((count, s.X), 1)
        a = lookup(place - col + R, fine, 2)
        b = 0.5 * lookup((place + E) // 2 - R - col // 2 + R, coarse, 2)
        blocks.append(wide([a, b]).astype(BF16))

    block(iota((s.X, s.X), 0), s.X)
    for kind in s.kx:
        c = iota((s.V * E, s.X), 0) % E
        block(jnp.where(upper(gx, kind), s.X + c, c - E), s.V * E)
    return jnp.concatenate(blocks, axis=0)


def xpass_kernel(s, *refs):
    fine, coarse, field, *refs = refs
    n, m = len(s.kx), len(s.kz)
    halos, refs = refs[:n], refs[n:]
    faces, refs = refs[:m], refs[m:]
    corners, refs = refs[:m], refs[m:]
    own, refs = refs[0], refs[1:]
    sides, packs = refs[:m], refs[m:]
    weights = x_weights(s, fine, coarse)
    lane_v = iota((1, s.V * E), 1) // E
    halo_all = [
        jnp.concatenate([h[: s.rows, :]] + [c[i * s.face : (i + 1) * s.face, :] for c in corners], axis=0)
        for i, h in enumerate(halos)
    ]
    for v in range(s.V):
        at = slice(v * s.X, (v + 1) * s.X)
        data = jnp.concatenate([field[v].reshape(s.rows, s.X)] + [f[v] for f in faces], axis=0)
        masked = [jnp.where(lane_v == v, h, jnp.zeros_like(h)) for h in halo_all]
        passed = dot(wide([data] + masked), weights).astype(BF16)
        own[: s.rows, at] = passed[: s.rows, : s.X]
        own[s.rows :, at] = passed[: s.rows, s.X :]
        for i, side in enumerate(sides):
            base = s.rows + i * s.face
            side[: s.raw, at] = passed[base : base + s.raw, : s.X]
            side[s.raw :, at] = passed[base : base + s.face, s.X :]
    gy = lax.axis_index("gy")
    half = s.Y // 2
    for kind, pack in zip(s.ky, packs):
        up = upper(gy, kind)
        y0 = jnp.where(up, s.Y - R, 0)
        c0 = jnp.where(up, half - R, 0)
        r, c = iota((s.yf, s.rows), 0), iota((s.yf, s.rows), 1)
        pick = one((c // s.Y == r // R) & (c % s.Y == y0 + r % R))
        pack[: s.yf, :] = dot(pick, own[: s.rows, :]).astype(BF16)
        r, c = iota((s.yc, s.rows), 0), iota((s.yc, s.rows), 1)
        pick = one((c // s.Y // 2 == r // R) & (c % s.Y // 2 == c0 + r % R), 0.25)
        at = s.yf
        pack[at : at + s.yc, :] = dot(pick, own[s.rows :, :]).astype(BF16)
        at += s.yc
        for side in sides:
            r, c = iota((s.zyf, s.raw), 0), iota((s.zyf, s.raw), 1)
            pick = one((c // s.Y == r // R) & (c % s.Y == y0 + r % R))
            pack[at : at + s.zyf, :] = dot(pick, side[: s.raw, :]).astype(BF16)
            at += s.zyf
            r, c = iota((s.zyc, s.face), 0), iota((s.zyc, s.face), 1)
            q, j = r // R, r % R
            near = (c < s.raw) & (c // s.Y // 2 == q) & (c % s.Y // 2 == c0 + j)
            b = c - s.raw
            far = (c >= s.raw) & (b // half + R // 2 == q) & (b % half == c0 + j)
            pick = jnp.where(near, 0.25, jnp.where(far, 1.0, 0.0)).astype(BF16)
            pack[at : at + s.zyc, :] = dot(pick, side[s.raw :, :]).astype(BF16)
            at += s.zyc


def yz_weights(s, fine, coarse):
    gy, gz = lax.axis_index("gy"), lax.axis_index("gz")
    half, deep = s.Y // 2, s.Z // 2
    blocks = []

    def block(taps, z, y, div, scale=None):
        count = z.shape[1]
        a = lookup(z - iota((s.Z, count), 0) // div + R, taps, 0)
        b = lookup(y - iota((s.Y, count), 0) // div + R, taps, 1)
        if scale is not None:
            b = b * scale
        both = a.reshape(s.Z, 1, count) * b.reshape(1, s.Y, count)
        blocks.append(both.reshape(s.rows, count).astype(BF16))

    c = iota((1, s.rows), 1)
    block(fine, c // s.Y, c % s.Y, 1)
    block(coarse, c // s.Y // 2, c % s.Y // 2, 2, 0.25)
    for kind in s.kz:
        up = upper(gz, kind)
        c = iota((1, s.raw), 1)
        block(fine, c // s.Y + jnp.where(up, s.Z, -R), c % s.Y, 1)
        c = iota((1, s.face), 1)
        b = c - s.raw
        near = c // s.Y // 2 + jnp.where(up, deep, -R // 2)
        far = b // half + jnp.where(up, deep + R // 2, -R)
        z = jnp.where(c < s.raw, near, far)
        y = jnp.where(c < s.raw, c % s.Y // 2, b % half)
        block(coarse, z, y, 2, jnp.where(c < s.raw, 0.25, 1.0))
    for kind in s.ky:
        up = upper(gy, kind)
        fy, cy = jnp.where(up, s.Y, -R), jnp.where(up, half, -R)
        c = iota((1, s.yf), 1)
        block(fine, c // R, c % R + fy, 1)
        c = iota((1, s.yc), 1)
        block(coarse, c // R, c % R + cy, 2)
        for zkind in s.kz:
            zup = upper(gz, zkind)
            c = iota((1, s.zyf), 1)
            block(fine, c // R + jnp.where(zup, s.Z, -R), c % R + fy, 1)
            q = iota((1, s.zyc), 1) // R
            j = iota((1, s.zyc), 1) % R
            near = q + jnp.where(zup, deep, -R // 2)
            far = q - R // 2 + jnp.where(zup, deep + R // 2, -R)
            block(coarse, jnp.where(q < R // 2, near, far), j + cy, 2)
    r, c = iota((s.rows, s.top), 0), iota((s.rows, s.top), 1)
    z, y = r // s.Y // (s.Z // s.tz), r % s.Y // (s.Y // s.ty)
    blocks.append(one((c // s.tx == z * s.ty + y)))
    return blocks


def final_kernel(s, *refs):
    fine, coarse, own, *refs = refs
    m, k = len(s.kz), len(s.ky)
    sides, refs = refs[:m], refs[m:]
    packs, refs = refs[:k], refs[k:]
    gathered, kernel, out, weights = refs
    at = 0
    for block in yz_weights(s, fine, coarse):
        weights[:, at : at + block.shape[1]] = block
        at += block.shape[1]
    total = jnp.zeros((s.top, s.V), F32)
    for z in range(s.nz):
        for i in range(s.tz):
            for y in range(s.ny):
                part = jnp.zeros((s.V, s.tile), F32)
                for x in range(s.nx):
                    device = (x * s.ny + y) * s.nz + z
                    part = part + gathered[device, i * s.V : (i + 1) * s.V, :].astype(F32)
                q = ((z * s.tz + i) * s.ny + y) * s.tile
                total = total + dot(kernel[:, q : q + s.tile], part.astype(BF16), ((1,), (1,)))
    r, c = iota((s.top, s.X), 0), iota((s.top, s.X), 1)
    spread = c // (s.X // s.tx) == r % s.tx
    for v in range(s.V):
        cols = slice(v * s.X, (v + 1) * s.X)
        line = jnp.broadcast_to(total[:, v : v + 1], (s.top, s.X))
        top = jnp.where(spread, line, 0.0).astype(BF16)
        parts = [own[:, cols]] + [x[:, cols] for x in sides] + [x[:, cols] for x in packs] + [top]
        result = dot(weights[...], jnp.concatenate(parts, axis=0))
        out[v] = result.astype(BF16).reshape(s.Z, s.Y, s.X)


def shape(*dims):
    return jax.ShapeDtypeStruct(dims, BF16)


def bind(body, s):
    def kernel(*refs):
        body(s, *refs)

    kernel.__name__ = body.__name__
    return kernel


def shards(sizes, field, fine_taps, coarse_taps, top_kernel):
    s = Sizes(field.shape, top_kernel.shape[:3], sizes)
    n, m, k = len(s.kx), len(s.kz), len(s.ky)

    def run(body, arrays, outs, scalars=0, scratch=(), flops=0, nbytes=2 << 20):
        return pl.pallas_call(
            bind(body, s),
            name=body.__name__,
            out_shape=outs,
            in_specs=[smem()] * scalars + [vmem()] * (len(arrays) - scalars),
            out_specs=[vmem()] * len(outs),
            scratch_shapes=scratch,
            cost_estimate=pl.CostEstimate(flops=flops, bytes_accessed=nbytes, transcendentals=0),
        )(*arrays)

    faces = run(faces_kernel, [field], [shape(s.V, s.face, s.X)] * m)
    faces = [lax.ppermute(a, "gz", swaps(s.nz, kind)) for a, kind in zip(faces, s.kz)]
    *edges, piece = run(
        edges_kernel, [field], [shape(s.rows + 2 * s.avg, s.V * E)] * n + [shape(s.tz * s.V, s.tile)]
    )
    halos = [lax.ppermute(a, "gx", swaps(s.nx, kind)) for a, kind in zip(edges, s.kx)]
    corners = run(corners_kernel, halos, [shape(n * s.face, s.V * E)] * m)
    corners = [lax.ppermute(a, "gz", swaps(s.nz, kind)) for a, kind in zip(corners, s.kz)]
    devices = s.nx * s.ny * s.nz
    gathered = lax.all_to_all(
        jnp.broadcast_to(piece, (devices,) + piece.shape), ("gx", "gy", "gz"), 0, 0
    )
    own, *rest = run(
        xpass_kernel,
        [fine_taps, coarse_taps, field] + halos + faces + corners,
        [shape(2 * s.rows, s.lanes)] + [shape(s.gz, s.lanes)] * m + [shape(s.ypack, s.lanes)] * k,
        scalars=2,
    )
    sides, packs = rest[:m], rest[m:]
    packs = [lax.ppermute(a, "gy", swaps(s.ny, kind)) for a, kind in zip(packs, s.ky)]
    depth = 2 * s.rows + m * s.gz + k * s.ypack + s.top
    kernel_rows = top_kernel.reshape(s.top, top_kernel.shape[3])
    return run(
        final_kernel,
        [fine_taps, coarse_taps, own] + sides + packs + [gathered, kernel_rows],
        [shape(*field.shape)],
        scalars=2,
        scratch=[pltpu.VMEM((s.rows, depth), BF16)],
    )[0]


def solution(mesh):
    sizes = tuple(mesh.shape[name] for name in ("gx", "gy", "gz"))

    def body(*args):
        return shards(sizes, *args)

    return jax.shard_map(
        body,
        mesh=mesh,
        in_specs=(P(None, "gz", "gy", "gx"), P(), P(), P("gz", "gy", "gx", None)),
        out_specs=P(None, "gz", "gy", "gx"),
        check_vma=False,
    )
```

```python
import jax
import jax.numpy as jnp
from jax import lax
from jax.experimental import pallas as pl
from jax.experimental.pallas import tpu as pltpu
from jax.sharding import PartitionSpec as P

F32 = jnp.float32
BF16 = jnp.bfloat16
R = 4
E = 2 * R


def swaps(count, kind):
    pairs = []
    for i in range(kind, count - 1, 2):
        pairs += [(i, i + 1), (i + 1, i)]
    return pairs


def kinds(count):
    return [k for k in (0, 1) if swaps(count, k)]


def upper(index, kind):
    return lax.rem(index + kind, 2) == 0


def iota(shape, dim):
    return lax.broadcasted_iota(jnp.int32, shape, dim)


def dot(a, b, dims=((1,), (0,)), precision=None):
    return lax.dot_general(a, b, (dims, ((), ())), precision=precision, preferred_element_type=F32)


def lookup(offset, taps, row):
    total = jnp.zeros(offset.shape, F32)
    for k in range(2 * R + 1):
        total = jnp.where(offset == k, taps[row, k], total)
    return total


def one(condition, value=1.0):
    return jnp.where(condition, value, 0.0).astype(BF16)


def wide(parts):
    return jnp.concatenate(parts, axis=1)


class Sizes:
    def __init__(self, shape, top_shape, mesh_sizes):
        self.V, self.Z, self.Y, self.X = shape
        self.nx, self.ny, self.nz = mesh_sizes
        self.rows = self.Z * self.Y
        self.lanes = self.V * self.X
        self.raw = R * self.Y
        self.avg = (R // 2) * (self.Y // 2)
        self.face = self.raw + self.avg
        self.kx, self.ky, self.kz = kinds(self.nx), kinds(self.ny), kinds(self.nz)
        self.yf, self.yc = self.Z * R, (self.Z // 2) * R
        self.zyf, self.zyc = R * R, R * R
        self.tz, self.ty, self.tx = top_shape
        self.top = self.tz * self.ty * self.tx
        self.gz = self.raw + self.face
        self.tile = self.ty * self.tx * self.nx


def smem():
    return pl.BlockSpec(memory_space=pltpu.SMEM)


def vmem():
    return pl.BlockSpec(memory_space=pltpu.VMEM)


def faces_kernel(s, field, *refs):
    me = lax.axis_index("gz")
    halos, outs = refs[: len(s.kx)], refs[len(s.kx) :]
    row = iota((s.avg, s.raw), 0)
    col = iota((s.avg, s.raw), 1)
    half = s.Y // 2
    mean = one((col // s.Y // 2 == row // half) & (col % s.Y // 2 == row % half), 0.25)
    for kind, out in zip(s.kz, outs):
        up = upper(me, kind)
        start = jnp.where(up, s.Z - R, 0)
        further = jnp.where(up, s.Z - E, R)
        for v in range(s.V):
            out[v * s.face : v * s.face + s.raw, :] = field[v, pl.ds(start, R)].reshape(s.raw, s.X)
        data = wide([field[v, pl.ds(further, R)].reshape(s.raw, s.X) for v in range(s.V)])
        means = dot(mean, data).astype(BF16)
        for v in range(s.V):
            out[v * s.face + s.raw : (v + 1) * s.face, :] = means[:, v * s.X : (v + 1) * s.X]
        row0 = pl.multiple_of(jnp.where(up, s.rows - s.raw, 0), 16)
        mean0 = pl.multiple_of(jnp.where(up, s.rows + s.avg, s.rows), 16)
        at = s.V * s.face
        for halo in halos:
            out[at : at + s.raw, :] = halo[pl.ds(row0, s.raw), :]
            out[at + s.raw : at + s.face, :] = halo[pl.ds(mean0, s.avg), :]
            at += s.face


def edges_kernel(s, field, *outs):
    gx = lax.axis_index("gx")
    *edges, piece = outs
    data = wide([field[v].reshape(s.rows, s.X) for v in range(s.V)])
    row = iota((s.lanes, s.V * E), 0)
    lane = iota((s.lanes, s.V * E), 1)
    half = s.Y // 2
    for kind, out in zip(s.kx, edges):
        first = jnp.where(upper(gx, kind), s.X - E, 0)
        pick = one((row // s.X == lane // E) & (row % s.X - first == lane % E))
        packed = dot(data, pick).astype(BF16)
        out[: s.rows, :] = packed
        r = iota((2 * s.avg, s.rows), 0)
        c = iota((2 * s.avg, s.rows), 1)
        layer = r // half * 2 + jnp.where(r < s.avg, R, s.Z - E - R)
        mean = one((c // s.Y // 2 * 2 == layer) & (c % s.Y // 2 == r % half), 0.25)
        out[s.rows :, :] = dot(mean, packed).astype(BF16)
    deep, tall, long = s.Z // s.tz, s.Y // s.ty, s.X // s.tx
    r = iota((8, s.rows), 0)
    c = iota((8, s.rows), 1)
    pool = one(c // s.Y // deep * s.ty + c % s.Y // tall == r, 1.0 / (deep * tall))
    sums = dot(pool, data)
    sub = iota((s.V, s.X), 0)
    x = iota((s.X, s.tile), 0)
    lane = iota((s.X, s.tile), 1)
    for i in range(s.tz):
        total = jnp.zeros((s.V, s.tile), F32)
        for j in range(s.ty):
            p = i * s.ty + j
            by_vector = jnp.zeros((s.V, s.X), F32)
            for v in range(s.V):
                line = jnp.broadcast_to(sums[p : p + 1, v * s.X : (v + 1) * s.X], (s.V, s.X))
                by_vector = jnp.where(sub == v, line, by_vector)
            spread = jnp.where(lane == (j * s.nx + gx) * s.tx + x // long, 1.0 / long, 0.0)
            total = total + dot(by_vector, spread, precision=lax.Precision.HIGHEST)
        piece[i * s.V : (i + 1) * s.V, :] = total.astype(BF16)


def x_weights(s, fine, coarse):
    gx = lax.axis_index("gx")
    blocks = []

    def block(place, count):
        col = iota((count, s.X), 1)
        a = lookup(place - col + R, fine, 2)
        b = 0.5 * lookup((place + E) // 2 - R - col // 2 + R, coarse, 2)
        blocks.append(wide([a, b]).astype(BF16))

    block(iota((s.X, s.X), 0), s.X)
    for kind in s.kx:
        c = iota((s.V * E, s.X), 0) % E
        block(jnp.where(upper(gx, kind), s.X + c, c - E), s.V * E)
    return jnp.concatenate(blocks, axis=0)


def pick_y(s, up, fine):
    if fine:
        r, c = iota((s.yf, s.rows), 0), iota((s.yf, s.rows), 1)
        y0 = jnp.where(up, s.Y - R, 0)
        return one((c // s.Y == r // R) & (c % s.Y == y0 + r % R))
    r, c = iota((s.yc, s.rows), 0), iota((s.yc, s.rows), 1)
    c0 = jnp.where(up, s.Y // 2 - R, 0)
    return one((c // s.Y // 2 == r // R) & (c % s.Y // 2 == c0 + r % R), 0.25)


def pick_zy(s, up, fine):
    half = s.Y // 2
    if fine:
        r, c = iota((s.zyf, s.raw), 0), iota((s.zyf, s.raw), 1)
        y0 = jnp.where(up, s.Y - R, 0)
        return one((c // s.Y == r // R) & (c % s.Y == y0 + r % R))
    r, c = iota((s.zyc, s.face), 0), iota((s.zyc, s.face), 1)
    q, y = r // R, r % R + jnp.where(up, half - R, 0)
    near = (c < s.raw) & (c // s.Y // 2 == q) & (c % s.Y // 2 == y)
    b = c - s.raw
    far = (c >= s.raw) & (b // half + R // 2 == q) & (b % half == y)
    return jnp.where(near, 0.25, jnp.where(far, 1.0, 0.0)).astype(BF16)


def xpass(s, weights, data, halos, v):
    lane_v = iota((1, s.V * E), 1) // E
    masked = [jnp.where(lane_v == v, h, jnp.zeros_like(h)) for h in halos]
    return dot(wide([data] + masked), weights).astype(BF16)


def own_kernel(s, *refs):
    fine, coarse, field, *refs = refs
    n = len(s.kx)
    halos, (weights, own, *packs) = [h[: s.rows, :] for h in refs[:n]], refs[n:]
    weights[...] = x_weights(s, fine, coarse)
    for v in range(s.V):
        at = slice(v * s.X, (v + 1) * s.X)
        passed = xpass(s, weights[...], field[v].reshape(s.rows, s.X), halos, v)
        own[: s.rows, at] = passed[:, : s.X]
        own[s.rows :, at] = passed[:, s.X :]
    gy = lax.axis_index("gy")
    for kind, pack in zip(s.ky, packs):
        up = upper(gy, kind)
        pack[: s.yf, :] = dot(pick_y(s, up, True), own[: s.rows, :]).astype(BF16)
        pack[s.yf :, :] = dot(pick_y(s, up, False), own[s.rows :, :]).astype(BF16)


def sides_kernel(s, weights, *refs):
    m = len(s.kz)
    faces, sides, packs = refs[:m], refs[m : 2 * m], refs[2 * m :]
    base = s.V * s.face
    halos = [
        jnp.concatenate([f[base + i * s.face : base + (i + 1) * s.face, :] for f in faces], axis=0)
        for i in range(len(s.kx))
    ]
    for v in range(s.V):
        at = slice(v * s.X, (v + 1) * s.X)
        data = jnp.concatenate([f[v * s.face : (v + 1) * s.face, :] for f in faces], axis=0)
        passed = xpass(s, weights[...], data, halos, v)
        for i, side in enumerate(sides):
            base = i * s.face
            side[: s.raw, at] = passed[base : base + s.raw, : s.X]
            side[s.raw :, at] = passed[base : base + s.face, s.X :]
    gy = lax.axis_index("gy")
    for kind, pack in zip(s.ky, packs):
        up = upper(gy, kind)
        at = 0
        for side in sides:
            pack[at : at + s.zyf, :] = dot(pick_zy(s, up, True), side[: s.raw, :]).astype(BF16)
            at += s.zyf
            pack[at : at + s.zyc, :] = dot(pick_zy(s, up, False), side[s.raw :, :]).astype(BF16)
            at += s.zyc


def yz_weights(s, fine, coarse):
    gy, gz = lax.axis_index("gy"), lax.axis_index("gz")
    half, deep = s.Y // 2, s.Z // 2

    def block(taps, z, y, div, scale=None):
        count = z.shape[1]
        a = lookup(z - iota((s.Z, count), 0) // div + R, taps, 0)
        b = lookup(y - iota((s.Y, count), 0) // div + R, taps, 1)
        if scale is not None:
            b = b * scale
        both = a.reshape(s.Z, 1, count) * b.reshape(1, s.Y, count)
        return both.reshape(s.rows, count).astype(BF16)

    c = iota((1, s.rows), 1)
    first = [
        block(fine, c // s.Y, c % s.Y, 1),
        block(coarse, c // s.Y // 2, c % s.Y // 2, 2, 0.25),
    ]
    second = []
    for kind in s.ky:
        up = upper(gy, kind)
        c = iota((1, s.yf), 1)
        first.append(block(fine, c // R, c % R + jnp.where(up, s.Y, -R), 1))
        c = iota((1, s.yc), 1)
        first.append(block(coarse, c // R, c % R + jnp.where(up, half, -R), 2))
    for kind in s.kz:
        up = upper(gz, kind)
        c = iota((1, s.raw), 1)
        second.append(block(fine, c // s.Y + jnp.where(up, s.Z, -R), c % s.Y, 1))
        c = iota((1, s.face), 1)
        b = c - s.raw
        near = c // s.Y // 2 + jnp.where(up, deep, -R // 2)
        far = b // half + jnp.where(up, deep + R // 2, -R)
        z = jnp.where(c < s.raw, near, far)
        y = jnp.where(c < s.raw, c % s.Y // 2, b % half)
        second.append(block(coarse, z, y, 2, jnp.where(c < s.raw, 0.25, 1.0)))
    for kind in s.ky:
        up = upper(gy, kind)
        for zkind in s.kz:
            zup = upper(gz, zkind)
            c = iota((1, s.zyf), 1)
            z, y = c // R + jnp.where(zup, s.Z, -R), c % R + jnp.where(up, s.Y, -R)
            second.append(block(fine, z, y, 1))
            c = iota((1, s.zyc), 1)
            q = c // R
            near = q + jnp.where(zup, deep, -R // 2)
            far = q - R // 2 + jnp.where(zup, deep + R // 2, -R)
            z, y = jnp.where(q < R // 2, near, far), c % R + jnp.where(up, half, -R)
            second.append(block(coarse, z, y, 2))
    r, c = iota((s.rows, s.top), 0), iota((s.rows, s.top), 1)
    z, y = r // s.Y // (s.Z // s.tz), r % s.Y // (s.Y // s.ty)
    second.append(one(c // s.tx == z * s.ty + y))
    return first, second


def partial_kernel(s, *refs):
    fine, coarse, own, *refs = refs
    k = len(s.ky)
    packs, (total, later, now) = refs[:k], refs[k:]
    first, second = yz_weights(s, fine, coarse)
    for ref, blocks in ((now, first), (later, second)):
        at = 0
        for block in blocks:
            ref[:, at : at + block.shape[1]] = block
            at += block.shape[1]
    step = min(s.lanes, 4 * s.X)
    for at in range(0, s.lanes, step):
        cols = slice(at, at + step)
        parts = [own[:, cols]] + [x[:, cols] for x in packs]
        total[:, cols] = dot(now[...], jnp.concatenate(parts, axis=0))


def final_kernel(s, *refs):
    m, k = len(s.kz), len(s.ky)
    partial, later, *refs = refs
    sides, refs = refs[:m], refs[m:]
    packs, refs = refs[:k], refs[k:]
    gathered, kernel, out = refs
    gy, gz = lax.axis_index("gy"), lax.axis_index("gz")
    total = jnp.zeros((s.top, s.V), F32)
    for z in range(s.nz):
        for y in range(s.ny):
            for i in range(s.tz):
                part = gathered[slot(z, gz, s.nz), slot(y, gy, s.ny), i * s.V : (i + 1) * s.V, :]
                q = ((z * s.tz + i) * s.ny + y) * s.tile
                total = total + dot(kernel[:, q : q + s.tile], part, ((1,), (1,)))
    r, c = iota((s.top, s.X), 0), iota((s.top, s.X), 1)
    spread = c // (s.X // s.tx) == r % s.tx
    for v in range(s.V):
        cols = slice(v * s.X, (v + 1) * s.X)
        line = jnp.broadcast_to(total[:, v : v + 1], (s.top, s.X))
        top = jnp.where(spread, line, 0.0).astype(BF16)
        parts = [x[:, cols] for x in sides] + [x[:, cols] for x in packs] + [top]
        result = dot(later[...], jnp.concatenate(parts, axis=0)) + partial[:, cols]
        out[v] = result.astype(BF16).reshape(s.Z, s.Y, s.X)


def doubling(count):
    return count & (count - 1) == 0


def slot(index, me, count):
    return index ^ me if doubling(count) else index


def gather(a, axis, count, join):
    if not doubling(count):
        return join(list(lax.all_gather(a, axis)))
    step = 1
    while step < count:
        a = join([a, lax.ppermute(a, axis, [(i, i ^ step) for i in range(count)])])
        step *= 2
    return a


def shape(*dims):
    return jax.ShapeDtypeStruct(dims, BF16)


def bind(body, s):
    def kernel(*refs):
        body(s, *refs)

    kernel.__name__ = body.__name__
    return kernel


def shards(sizes, field, fine_taps, coarse_taps, top_kernel):
    s = Sizes(field.shape, top_kernel.shape[:3], sizes)
    n, m, k = len(s.kx), len(s.kz), len(s.ky)
    taps = [fine_taps, coarse_taps]

    def run(body, arrays, outs, scalars=0, scratch=(), flops=0, nbytes=1 << 20):
        call = pl.pallas_call(
            bind(body, s),
            name=body.__name__,
            out_shape=outs,
            in_specs=[smem()] * scalars + [vmem()] * (len(arrays) - scalars),
            out_specs=[vmem()] * len(outs),
            scratch_shapes=scratch,
            compiler_params=pltpu.CompilerParams(vmem_limit_bytes=24 << 20),
            cost_estimate=pl.CostEstimate(flops=flops, bytes_accessed=nbytes, transcendentals=0),
        )
        return list(call(*arrays))

    def swap(arrays, axis, count, which):
        return [lax.ppermute(a, axis, swaps(count, kind)) for a, kind in zip(arrays, which)]

    *edges, piece = run(
        edges_kernel, [field], [shape(s.rows + 2 * s.avg, s.V * E)] * n + [shape(s.tz * s.V, s.tile)]
    )
    stack = lambda parts: jnp.concatenate(parts, axis=0)
    known = gather(piece[None], "gy", s.ny, stack)
    halos = swap(edges, "gx", s.nx, s.kx)
    faces = run(faces_kernel, [field] + halos, [shape((s.V + n) * s.face, s.X)] * m)
    faces = swap(faces, "gz", s.nz, s.kz)
    known = gather(known, "gx", s.nx, sum)
    known = gather(known[None], "gz", s.nz, stack)
    x_depth = s.X + n * s.V * E
    weights, own, *packs = run(
        own_kernel,
        taps + [field] + halos,
        [shape(x_depth, 2 * s.X), shape(2 * s.rows, s.lanes)] + [shape(s.yf + s.yc, s.lanes)] * k,
        scalars=2,
    )
    packs = swap(packs, "gy", s.ny, s.ky)
    now = 2 * s.rows + k * (s.yf + s.yc)
    later = m * s.gz + k * m * (s.zyf + s.zyc) + s.top
    partial, w_later = run(
        partial_kernel,
        taps + [own] + packs,
        [jax.ShapeDtypeStruct((s.rows, s.lanes), F32), shape(s.rows, later)],
        scalars=2,
        scratch=[pltpu.VMEM((s.rows, now), BF16)],
    )
    rest = run(
        sides_kernel,
        [weights] + faces,
        [shape(s.gz, s.lanes)] * m + [shape(m * (s.zyf + s.zyc), s.lanes)] * k,
    )
    sides, packs = rest[:m], swap(rest[m:], "gy", s.ny, s.ky)
    kernel_rows = top_kernel.reshape(s.top, top_kernel.shape[3])
    return run(
        final_kernel,
        [partial, w_later] + sides + packs + [known, kernel_rows],
        [shape(*field.shape)],
    )[0]


def solution(mesh):
    sizes = tuple(mesh.shape[name] for name in ("gx", "gy", "gz"))

    def body(*args):
        return shards(sizes, *args)

    return jax.shard_map(
        body,
        mesh=mesh,
        in_specs=(P(None, "gz", "gy", "gx"), P(), P(), P("gz", "gy", "gx", None)),
        out_specs=P(None, "gz", "gy", "gx"),
        check_vma=False,
    )
```

```python
import jax
import jax.numpy as jnp
from jax import lax
from jax.experimental import pallas as pl
from jax.experimental.pallas import tpu as pltpu
from jax.sharding import PartitionSpec as P

F32 = jnp.float32
BF16 = jnp.bfloat16
R = 4
E = 2 * R


def swaps(count, kind, ring=False):
    pairs = []
    for i in range(kind, count - 1, 2):
        pairs += [(i, i + 1), (i + 1, i)]
    if ring and kind == 1 and pairs and count % 2 == 0:
        pairs += [(0, count - 1), (count - 1, 0)]
    return pairs


def partner_missing(index, count, kind):
    at = index + jnp.where(upper(index, kind), 1, -1)
    return (at < 0) | (at >= count)


def kinds(count):
    return [k for k in (0, 1) if swaps(count, k)]


def upper(index, kind):
    return lax.rem(index + kind, 2) == 0


def iota(shape, dim):
    return lax.broadcasted_iota(jnp.int32, shape, dim)


def dot(a, b, dims=((1,), (0,)), precision=None):
    return lax.dot_general(a, b, (dims, ((), ())), precision=precision, preferred_element_type=F32)


def lookup(offset, taps, row):
    total = jnp.zeros(offset.shape, F32)
    for k in range(2 * R + 1):
        total = jnp.where(offset == k, taps[row, k], total)
    return total


def one(condition, value=1.0):
    return jnp.where(condition, value, 0.0).astype(BF16)


def wide(parts):
    return jnp.concatenate(parts, axis=1)


class Sizes:
    def __init__(self, shape, top_shape, mesh_sizes):
        self.V, self.Z, self.Y, self.X = shape
        self.nx, self.ny, self.nz = mesh_sizes
        self.rows = self.Z * self.Y
        self.lanes = self.V * self.X
        self.raw = R * self.Y
        self.avg = (R // 2) * (self.Y // 2)
        self.face = self.raw + self.avg
        self.kx, self.ky, self.kz = kinds(self.nx), kinds(self.ny), kinds(self.nz)
        self.yf, self.yc = self.Z * R, (self.Z // 2) * R
        self.zyf, self.zyc = R * R, R * R
        self.tz, self.ty, self.tx = top_shape
        self.top = self.tz * self.ty * self.tx
        self.gz = self.raw + self.face
        self.tile = self.ty * self.tx * self.nx
        self.ride = self.nx == 4 and self.nz == 4 and self.tile == self.V * E
        self.edge = self.rows + 2 * self.avg + (self.tz * self.V if self.ride else 0)
        self.chunks = 4 if self.V % 4 == 0 else 1
        self.corner = len(self.kx) * self.face + (self.tz * self.V if self.ride else 0)


def smem():
    return pl.BlockSpec(memory_space=pltpu.SMEM)


def vmem():
    return pl.BlockSpec(memory_space=pltpu.VMEM)


def faces_kernel(s, field, *outs):
    me = lax.axis_index("gz")
    row = iota((s.avg, s.raw), 0)
    col = iota((s.avg, s.raw), 1)
    half = s.Y // 2
    mean = one((col // s.Y // 2 == row // half) & (col % s.Y // 2 == row % half), 0.25)
    for kind, out in zip(s.kz, outs):
        up = upper(me, kind)
        start = jnp.where(up, s.Z - R, 0)
        further = jnp.where(up, s.Z - E, R)
        for v in range(s.V):
            out[v, : s.raw, :] = field[v, pl.ds(start, R)].reshape(s.raw, s.X)
        data = wide([field[v, pl.ds(further, R)].reshape(s.raw, s.X) for v in range(s.V)])
        means = dot(mean, data).astype(BF16)
        for v in range(s.V):
            out[v, s.raw :, :] = means[:, v * s.X : (v + 1) * s.X]


def corners_kernel(s, *refs):
    me = lax.axis_index("gz")
    n = len(s.kx)
    halos, refs = refs[:n], refs[n:]
    if s.ride:
        piece, across, *outs, known = refs
        total = piece[...].astype(F32) + across[...].astype(F32)
        for halo in halos:
            total = total + halo[s.rows + 2 * s.avg :, :].astype(F32)
        known[...] = total.astype(BF16)
    else:
        outs = refs
    for kind, out in zip(s.kz, outs):
        up = upper(me, kind)
        start = pl.multiple_of(jnp.where(up, s.rows - s.raw, 0), 16)
        mean = pl.multiple_of(jnp.where(up, s.rows + s.avg, s.rows), 16)
        for i, halo in enumerate(halos):
            at = i * s.face
            out[at : at + s.raw, :] = halo[pl.ds(start, s.raw), :]
            out[at + s.raw : at + s.face, :] = halo[pl.ds(mean, s.avg), :]
        if s.ride:
            out[n * s.face :, :] = total.astype(BF16)


def edges_kernel(s, field, *refs):
    gx = lax.axis_index("gx")
    n = len(s.kx)
    edges, piece = refs[:n], refs[n]
    chunk = s.V // s.chunks
    half = s.Y // 2
    deep, tall, long = s.Z // s.tz, s.Y // s.ty, s.X // s.tx
    row = iota((chunk * s.X, s.V * E), 0)
    lane = iota((chunk * s.X, s.V * E), 1)
    own_v, own_x = row // s.X, row % s.X
    r, c = iota((8, s.rows), 0), iota((8, s.rows), 1)
    pool = one(c // s.Y // deep * s.ty + c % s.Y // tall == r, 1.0 / (deep * tall))
    sub = iota((s.V, s.X), 0)
    first = [jnp.where(upper(gx, kind), s.X - E, 0) for kind in s.kx]
    packed = [jnp.zeros((s.rows, s.V * E), F32) for kind in s.kx]
    by_vector = [jnp.zeros((s.V, s.X), F32) for _ in range(s.tz * s.ty)]
    for i in range(s.chunks):
        data = wide([field[v].reshape(s.rows, s.X) for v in range(i * chunk, (i + 1) * chunk)])
        for j in range(n):
            pick = one((own_v + i * chunk == lane // E) & (own_x - first[j] == lane % E))
            packed[j] = packed[j] + dot(data, pick)
        sums = dot(pool, data)
        for p in range(s.tz * s.ty):
            for v in range(chunk):
                line = jnp.broadcast_to(sums[p : p + 1, v * s.X : (v + 1) * s.X], (s.V, s.X))
                by_vector[p] = jnp.where(sub == v + i * chunk, line, by_vector[p])
    r, c = iota((2 * s.avg, s.rows), 0), iota((2 * s.avg, s.rows), 1)
    layer = r // half * 2 + jnp.where(r < s.avg, R, s.Z - E - R)
    mean = one((c // s.Y // 2 * 2 == layer) & (c % s.Y // 2 == r % half), 0.25)
    for j in range(n):
        edge = packed[j].astype(BF16)
        edges[j][: s.rows, :] = edge
        edges[j][s.rows : s.rows + 2 * s.avg, :] = dot(mean, edge).astype(BF16)
    x, lane = iota((s.X, s.tile), 0), iota((s.X, s.tile), 1)
    for i in range(s.tz):
        total = jnp.zeros((s.V, s.tile), F32)
        for j in range(s.ty):
            spread = jnp.where(lane == (j * s.nx + gx) * s.tx + x // long, 1.0 / long, 0.0)
            total = total + dot(by_vector[i * s.ty + j], spread, precision=lax.Precision.HIGHEST)
        total = total.astype(BF16)
        piece[i * s.V : (i + 1) * s.V, :] = total
        if s.ride:
            for edge in edges:
                at = s.rows + 2 * s.avg + i * s.V
                edge[at : at + s.V, :] = total


def x_weights(s, fine, coarse):
    gx = lax.axis_index("gx")
    blocks = []

    def block(place, count):
        col = iota((count, s.X), 1)
        a = lookup(place - col + R, fine, 2)
        b = 0.5 * lookup((place + E) // 2 - R - col // 2 + R, coarse, 2)
        blocks.append(wide([a, b]).astype(BF16))

    block(iota((s.X, s.X), 0), s.X)
    for kind in s.kx:
        c = iota((s.V * E, s.X), 0) % E
        place = jnp.where(upper(gx, kind), s.X + c, c - E)
        block(jnp.where(partner_missing(gx, s.nx, kind), -4 * s.X, place), s.V * E)
    return jnp.concatenate(blocks, axis=0)


def pick_y(s, up, fine):
    if fine:
        r, c = iota((s.yf, s.rows), 0), iota((s.yf, s.rows), 1)
        y0 = jnp.where(up, s.Y - R, 0)
        return one((c // s.Y == r // R) & (c % s.Y == y0 + r % R))
    r, c = iota((s.yc, s.rows), 0), iota((s.yc, s.rows), 1)
    c0 = jnp.where(up, s.Y // 2 - R, 0)
    return one((c // s.Y // 2 == r // R) & (c % s.Y // 2 == c0 + r % R), 0.25)


def pick_zy(s, up, fine):
    half = s.Y // 2
    if fine:
        r, c = iota((s.zyf, s.raw), 0), iota((s.zyf, s.raw), 1)
        y0 = jnp.where(up, s.Y - R, 0)
        return one((c // s.Y == r // R) & (c % s.Y == y0 + r % R))
    r, c = iota((s.zyc, s.face), 0), iota((s.zyc, s.face), 1)
    q, y = r // R, r % R + jnp.where(up, half - R, 0)
    near = (c < s.raw) & (c // s.Y // 2 == q) & (c % s.Y // 2 == y)
    b = c - s.raw
    far = (c >= s.raw) & (b // half + R // 2 == q) & (b % half == y)
    return jnp.where(near, 0.25, jnp.where(far, 1.0, 0.0)).astype(BF16)


def xpass(s, weights, data, halos, v):
    lane_v = iota((1, s.V * E), 1) // E
    masked = [jnp.where(lane_v == v, h, jnp.zeros_like(h)) for h in halos]
    return dot(wide([data] + masked), weights).astype(BF16)


def own_kernel(s, *refs):
    fine, coarse, field, *refs = refs
    n = len(s.kx)
    halos, (weights, own, *packs) = [h[: s.rows, :] for h in refs[:n]], refs[n:]
    weights[...] = x_weights(s, fine, coarse)
    for v in range(s.V):
        at = slice(v * s.X, (v + 1) * s.X)
        passed = xpass(s, weights[...], field[v].reshape(s.rows, s.X), halos, v)
        own[: s.rows, at] = passed[:, : s.X]
        own[s.rows :, at] = passed[:, s.X :]
    gy = lax.axis_index("gy")
    for kind, pack in zip(s.ky, packs):
        up = upper(gy, kind)
        pack[: s.yf, :] = dot(pick_y(s, up, True), own[: s.rows, :]).astype(BF16)
        pack[s.yf :, :] = dot(pick_y(s, up, False), own[s.rows :, :]).astype(BF16)


def sides_kernel(s, weights, *refs):
    m = len(s.kz)
    faces, corners, sides, packs = refs[:m], refs[m : 2 * m], refs[2 * m : 3 * m], refs[3 * m :]
    halos = [
        jnp.concatenate([c[i * s.face : (i + 1) * s.face, :] for c in corners], axis=0)
        for i in range(len(s.kx))
    ]
    for v in range(s.V):
        at = slice(v * s.X, (v + 1) * s.X)
        data = jnp.concatenate([f[v] for f in faces], axis=0)
        passed = xpass(s, weights[...], data, halos, v)
        for i, side in enumerate(sides):
            base = i * s.face
            side[: s.raw, at] = passed[base : base + s.raw, : s.X]
            side[s.raw :, at] = passed[base : base + s.face, s.X :]
    gy = lax.axis_index("gy")
    for kind, pack in zip(s.ky, packs):
        up = upper(gy, kind)
        at = 0
        for side in sides:
            pack[at : at + s.zyf, :] = dot(pick_zy(s, up, True), side[: s.raw, :]).astype(BF16)
            at += s.zyf
            pack[at : at + s.zyc, :] = dot(pick_zy(s, up, False), side[s.raw :, :]).astype(BF16)
            at += s.zyc


def yz_weights(s, fine, coarse):
    gy, gz = lax.axis_index("gy"), lax.axis_index("gz")
    half, deep = s.Y // 2, s.Z // 2

    def block(taps, z, y, div, scale=None):
        count = z.shape[1]
        a = lookup(z - iota((s.Z, count), 0) // div + R, taps, 0)
        b = lookup(y - iota((s.Y, count), 0) // div + R, taps, 1)
        if scale is not None:
            b = b * scale
        both = a.reshape(s.Z, 1, count) * b.reshape(1, s.Y, count)
        return both.reshape(s.rows, count).astype(BF16)

    c = iota((1, s.rows), 1)
    first = [
        block(fine, c // s.Y, c % s.Y, 1),
        block(coarse, c // s.Y // 2, c % s.Y // 2, 2, 0.25),
    ]
    second = []

    def zplace(kind, z):
        return jnp.where(partner_missing(gz, s.nz, kind), -4 * s.Z, z)

    for kind in s.ky:
        up = upper(gy, kind)
        c = iota((1, s.yf), 1)
        second.append(block(fine, c // R, c % R + jnp.where(up, s.Y, -R), 1))
        c = iota((1, s.yc), 1)
        second.append(block(coarse, c // R, c % R + jnp.where(up, half, -R), 2))
    for kind in s.kz:
        up = upper(gz, kind)
        c = iota((1, s.raw), 1)
        second.append(block(fine, zplace(kind, c // s.Y + jnp.where(up, s.Z, -R)), c % s.Y, 1))
        c = iota((1, s.face), 1)
        b = c - s.raw
        near = c // s.Y // 2 + jnp.where(up, deep, -R // 2)
        far = b // half + jnp.where(up, deep + R // 2, -R)
        z = zplace(kind, jnp.where(c < s.raw, near, far))
        y = jnp.where(c < s.raw, c % s.Y // 2, b % half)
        second.append(block(coarse, z, y, 2, jnp.where(c < s.raw, 0.25, 1.0)))
    for kind in s.ky:
        up = upper(gy, kind)
        for zkind in s.kz:
            zup = upper(gz, zkind)
            c = iota((1, s.zyf), 1)
            z, y = c // R + jnp.where(zup, s.Z, -R), c % R + jnp.where(up, s.Y, -R)
            second.append(block(fine, zplace(zkind, z), y, 1))
            c = iota((1, s.zyc), 1)
            q = c // R
            near = q + jnp.where(zup, deep, -R // 2)
            far = q - R // 2 + jnp.where(zup, deep + R // 2, -R)
            z, y = jnp.where(q < R // 2, near, far), c % R + jnp.where(up, half, -R)
            second.append(block(coarse, zplace(zkind, z), y, 2))
    r, c = iota((s.rows, s.top), 0), iota((s.rows, s.top), 1)
    z, y = r // s.Y // (s.Z // s.tz), r % s.Y // (s.Y // s.ty)
    second.append(one(c // s.tx == z * s.ty + y))
    return first, second


def partial_kernel(s, fine, coarse, own, total, later, now):
    first, second = yz_weights(s, fine, coarse)
    for ref, blocks in ((now, first), (later, second)):
        at = 0
        for block in blocks:
            ref[:, at : at + block.shape[1]] = block
            at += block.shape[1]
    step = min(s.lanes, 4 * s.X)
    for at in range(0, s.lanes, step):
        cols = slice(at, at + step)
        total[:, cols] = dot(now[...], own[:, cols])


def final_kernel(s, *refs):
    m, k = len(s.kz), len(s.ky)
    partial, later, *refs = refs
    ends, refs = refs[:k], refs[k:]
    sides, refs = refs[:m], refs[m:]
    packs, refs = refs[:k], refs[k:]
    gathered, kernel, out, held, sems = refs
    gy, gz = lax.axis_index("gy"), lax.axis_index("gz")
    total = jnp.zeros((s.top, s.V), F32)
    for z in range(s.nz):
        for y in range(s.ny):
            for i in range(s.tz):
                part = gathered[slot(y, gy, s.ny), slot(z, gz, s.nz), i * s.V : (i + 1) * s.V, :]
                q = ((z * s.tz + i) * s.ny + y) * s.tile
                total = total + dot(kernel[:, q : q + s.tile], part, ((1,), (1,)))
    r, c = iota((s.top, s.X), 0), iota((s.top, s.X), 1)
    spread = c // (s.X // s.tx) == r % s.tx
    chunk = s.V // s.chunks
    copies = []
    for v in range(s.V):
        cols = slice(v * s.X, (v + 1) * s.X)
        line = jnp.broadcast_to(total[:, v : v + 1], (s.top, s.X))
        top = jnp.where(spread, line, 0.0).astype(BF16)
        parts = [x[:, cols] for x in (*ends, *sides, *packs)] + [top]
        result = dot(later[...], jnp.concatenate(parts, axis=0)) + partial[:, cols]
        held[v] = result.astype(BF16).reshape(s.Z, s.Y, s.X)
        if v % chunk == chunk - 1:
            at = pl.ds(v + 1 - chunk, chunk)
            copies.append(pltpu.make_async_copy(held.at[at], out.at[at], sems.at[v // chunk]))
            copies[-1].start()
    for copy in copies:
        copy.wait()


def doubling(count):
    return count & (count - 1) == 0


def slot(index, me, count):
    return index ^ me if doubling(count) else index


def gather(a, axis, count, join):
    if not doubling(count):
        return join(list(lax.all_gather(a, axis)))
    step = 1
    while step < count:
        a = join([a, lax.ppermute(a, axis, [(i, i ^ step) for i in range(count)])])
        step *= 2
    return a


def shape(*dims):
    return jax.ShapeDtypeStruct(dims, BF16)


def bind(body, s):
    def kernel(*refs):
        body(s, *refs)

    kernel.__name__ = body.__name__
    return kernel


def shards(sizes, field, fine_taps, coarse_taps, top_kernel):
    s = Sizes(field.shape, top_kernel.shape[:3], sizes)
    n, m, k = len(s.kx), len(s.kz), len(s.ky)

    def run(body, arrays, outs, scalars=0, scratch=(), flops=0, far=(), far_out=False):
        specs = [vmem()] * len(arrays)
        for i in range(scalars):
            specs[i] = smem()
        for i in far:
            specs[i] = pl.BlockSpec(memory_space=pltpu.HBM)
        call = pl.pallas_call(
            bind(body, s),
            name=body.__name__,
            out_shape=outs,
            in_specs=specs,
            out_specs=[pl.BlockSpec(memory_space=pltpu.HBM) if far_out else vmem()] * len(outs),
            scratch_shapes=scratch,
            compiler_params=pltpu.CompilerParams(vmem_limit_bytes=24 << 20),
            cost_estimate=pl.CostEstimate(flops=flops, bytes_accessed=1 << 20, transcendentals=0),
        )
        return list(call(*arrays))

    def swap(arrays, axis, count, which, ring=False):
        return [lax.ppermute(a, axis, swaps(count, kind, ring)) for a, kind in zip(arrays, which)]

    taps = [fine_taps, coarse_taps]
    buffers = [pltpu.VMEM(field.shape, BF16), pltpu.SemaphoreType.DMA((s.chunks,))]
    top = shape(s.tz * s.V, s.tile)
    with jax.named_scope("faces"):
        faces = run(faces_kernel, [field], [shape(s.V, s.face, s.X)] * m)
    with jax.named_scope("zface"):
        faces = swap(faces, "gz", s.nz, s.kz)
    with jax.named_scope("edges"):
        *edges, piece = run(edges_kernel, [field], [shape(s.edge, s.V * E)] * n + [top])
    with jax.named_scope("xedge"):
        halos = swap(edges, "gx", s.nx, s.kx, s.ride)
    corner = [shape(s.corner, s.V * E)] * m
    stack = lambda parts: jnp.concatenate(parts, axis=0)
    if s.ride:
        with jax.named_scope("across"):
            across = lax.ppermute(piece, "gx", [(i, i ^ 2) for i in range(s.nx)])
        with jax.named_scope("corners"):
            *corners, known = run(corners_kernel, halos + [piece, across], corner + [top])
    else:
        with jax.named_scope("corners"):
            corners = run(corners_kernel, halos, corner)
    with jax.named_scope("zcorner"):
        corners = swap(corners, "gz", s.nz, s.kz, s.ride)
    if s.ride:
        with jax.named_scope("zacross"):
            across = lax.ppermute(known, "gz", [(i, i ^ 2) for i in range(s.nz)])
        near, far = [c[n * s.face :] for c in corners]
        known = jnp.stack([known, near, across, far])
    else:
        known = gather(gather(piece, "gx", s.nx, sum)[None], "gz", s.nz, stack)
    with jax.named_scope("known"):
        known = gather(known[None], "gy", s.ny, stack)
    x_depth = s.X + n * s.V * E
    with jax.named_scope("own"):
        weights, own, *ends = run(
            own_kernel,
            taps + [field] + halos,
            [shape(x_depth, 2 * s.X), shape(2 * s.rows, s.lanes)]
            + [shape(s.yf + s.yc, s.lanes)] * k,
            scalars=2,
            flops=4 * s.rows * s.V * x_depth * s.X,
        )
    with jax.named_scope("yown"):
        ends = swap(ends, "gy", s.ny, s.ky)
    later = k * (s.yf + s.yc) + m * s.gz + k * m * (s.zyf + s.zyc) + s.top
    with jax.named_scope("partial"):
        partial, w_later = run(
            partial_kernel,
            taps + [own],
            [jax.ShapeDtypeStruct((s.rows, s.lanes), F32), shape(s.rows, later)],
            scalars=2,
            scratch=[pltpu.VMEM((s.rows, 2 * s.rows), BF16)],
            flops=4 * s.rows * s.rows * s.lanes,
        )
    with jax.named_scope("sides"):
        rest = run(
            sides_kernel,
            [weights] + faces + corners,
            [shape(s.gz, s.lanes)] * m + [shape(m * (s.zyf + s.zyc), s.lanes)] * k,
        )
    with jax.named_scope("yside"):
        sides, packs = rest[:m], swap(rest[m:], "gy", s.ny, s.ky)
    kernel_rows = top_kernel.reshape(s.top, top_kernel.shape[3])
    with jax.named_scope("final"):
        return run(
            final_kernel,
            [partial, w_later] + ends + sides + packs + [known, kernel_rows],
            [shape(*field.shape)],
            scratch=buffers,
            far_out=True,
        )[0]


def solution(mesh):
    sizes = tuple(mesh.shape[name] for name in ("gx", "gy", "gz"))

    def body(*args):
        return shards(sizes, *args)

    return jax.shard_map(
        body,
        mesh=mesh,
        in_specs=(P(None, "gz", "gy", "gx"), P(), P(), P("gz", "gy", "gx", None)),
        out_specs=P(None, "gz", "gy", "gx"),
        check_vma=False,
    )
```

```python
import jax
import jax.numpy as jnp
from jax import lax
from jax.experimental import pallas as pl
from jax.experimental.pallas import tpu as pltpu
from jax.sharding import PartitionSpec as P


F32 = jnp.float32
BF16 = jnp.bfloat16
R = 4
E = 2 * R


def swaps(count, kind, ring=False):
    pairs = []
    for i in range(kind, count - 1, 2):
        pairs += [(i, i + 1), (i + 1, i)]
    if ring and kind == 1 and pairs and count % 2 == 0:
        pairs += [(0, count - 1), (count - 1, 0)]
    return pairs


def partner_missing(index, count, kind):
    at = index + jnp.where(upper(index, kind), 1, -1)
    return (at < 0) | (at >= count)


def kinds(count):
    return [k for k in (0, 1) if swaps(count, k)]


def upper(index, kind):
    return lax.rem(index + kind, 2) == 0


def iota(shape, dim):
    return lax.broadcasted_iota(jnp.int32, shape, dim)


def dot(a, b, dims=((1,), (0,)), precision=None):
    return lax.dot_general(a, b, (dims, ((), ())), precision=precision, preferred_element_type=F32)


def lookup(offset, taps, row):
    total = jnp.zeros(offset.shape, F32)
    for k in range(2 * R + 1):
        total = jnp.where(offset == k, taps[row, k], total)
    return total


def one(condition, value=1.0):
    return jnp.where(condition, value, 0.0).astype(BF16)


def wide(parts):
    return jnp.concatenate(parts, axis=1)


class Sizes:
    def __init__(self, shape, top_shape, mesh_sizes):
        self.V, self.Z, self.Y, self.X = shape
        self.nx, self.ny, self.nz = mesh_sizes
        self.rows = self.Z * self.Y
        self.lanes = self.V * self.X
        self.raw = R * self.Y
        self.avg = (R // 2) * (self.Y // 2)
        self.face = self.raw + self.avg
        self.kx, self.ky, self.kz = kinds(self.nx), kinds(self.ny), kinds(self.nz)
        self.yf, self.yc = self.Z * R, (self.Z // 2) * R
        self.zyf, self.zyc = R * R, R * R
        self.tz, self.ty, self.tx = top_shape
        self.top = self.tz * self.ty * self.tx
        self.gz = self.raw + self.face
        self.tile = self.ty * self.tx * self.nx
        self.ride = self.nx == 4 and self.nz == 4 and self.tile == self.V * E
        self.edge = self.rows + 2 * self.avg + (self.tz * self.V if self.ride else 0)
        self.ypack = len(self.kz) * (self.zyf + self.zyc)
        self.chunks = 4 if self.V % 4 == 0 else 1
        self.corner = len(self.kx) * self.face + (self.tz * self.V if self.ride else 0)


def smem():
    return pl.BlockSpec(memory_space=pltpu.SMEM)


def vmem():
    return pl.BlockSpec(memory_space=pltpu.VMEM)


def corners_kernel(s, *refs):
    me = lax.axis_index("gz")
    n = len(s.kx)
    halos, refs = refs[:n], refs[n:]
    if s.ride:
        piece, across, *outs, known = refs
        total = piece[...].astype(F32) + across[...].astype(F32)
        for halo in halos:
            total = total + halo[s.rows + 2 * s.avg :, :].astype(F32)
        known[...] = total.astype(BF16)
    else:
        outs = refs
    for kind, out in zip(s.kz, outs):
        up = upper(me, kind)
        start = pl.multiple_of(jnp.where(up, s.rows - s.raw, 0), 16)
        mean = pl.multiple_of(jnp.where(up, s.rows + s.avg, s.rows), 16)
        for i, halo in enumerate(halos):
            at = i * s.face
            out[at : at + s.raw, :] = halo[pl.ds(start, s.raw), :]
            out[at + s.raw : at + s.face, :] = halo[pl.ds(mean, s.avg), :]
        if s.ride:
            out[n * s.face :, :] = total.astype(BF16)


def front_kernel(s, field, *refs):
    gx = lax.axis_index("gx")
    n, m = len(s.kx), len(s.kz)
    faces, edges, (piece, held, sem) = refs[:m], refs[m : m + n], refs[m + n :]
    copy = pltpu.make_async_copy(field, held, sem)
    copy.start()
    half = s.Y // 2
    deep, tall, long = s.Z // s.tz, s.Y // s.ty, s.X // s.tx
    x, lane = iota((s.X, s.V * E), 0), iota((s.X, s.V * E), 1)
    picks = [one(x - jnp.where(upper(gx, kind), s.X - E, 0) == lane % E) for kind in s.kx]
    group = iota((1, s.V * E), 1) // E
    by_v = [
        wide([jnp.where(group == lane_group(s, j, v), p, jnp.zeros_like(p)) for j, p in enumerate(picks)])
        for v in range(s.V)
    ]
    sub = iota((s.V, s.X), 0)
    copy.wait()
    found = dot(
        wide([held[v].reshape(s.rows, s.X) for v in range(s.V)]), jnp.concatenate(by_v, axis=0)
    )
    by_vector = [jnp.zeros((s.V, s.X), F32) for _ in range(s.tz * s.ty)]
    for v in range(s.V):
        for i in range(s.tz):
            layers = held[v, i * deep].astype(F32)
            for z in range(i * deep + 1, (i + 1) * deep):
                layers = layers + held[v, z].astype(F32)
            for j in range(s.ty):
                line = jnp.sum(layers[j * tall : (j + 1) * tall], axis=0, keepdims=True)
                line = jnp.broadcast_to(line * (1.0 / (deep * tall)), (s.V, s.X))
                by_vector[i * s.ty + j] = jnp.where(sub == v, line, by_vector[i * s.ty + j])
    gz = lax.axis_index("gz")
    row = iota((s.avg, s.raw), 0)
    col = iota((s.avg, s.raw), 1)
    half = s.Y // 2
    mean = one((col // s.Y // 2 == row // half) & (col % s.Y // 2 == row % half), 0.25)
    for kind, out in zip(s.kz, faces):
        up = upper(gz, kind)
        start = jnp.where(up, s.Z - R, 0)
        further = jnp.where(up, s.Z - E, R)
        for v in range(s.V):
            out[v, : s.raw, :] = held[v, pl.ds(start, R)].reshape(s.raw, s.X)
        data = wide([held[v, pl.ds(further, R)].reshape(s.raw, s.X) for v in range(s.V)])
        means = dot(mean, data).astype(BF16)
        for v in range(s.V):
            out[v, s.raw :, :] = means[:, v * s.X : (v + 1) * s.X]
    r, c = iota((2 * s.avg, s.rows), 0), iota((2 * s.avg, s.rows), 1)
    layer = r // half * 2 + jnp.where(r < s.avg, R, s.Z - E - R)
    mean = one((c // s.Y // 2 * 2 == layer) & (c % s.Y // 2 == r % half), 0.25)
    for j in range(n):
        edge = found[:, j * s.V * E : (j + 1) * s.V * E].astype(BF16)
        edges[j][: s.rows, :] = edge
        edges[j][s.rows : s.rows + 2 * s.avg, :] = dot(mean, edge).astype(BF16)
    x, lane = iota((s.X, s.tile), 0), iota((s.X, s.tile), 1)
    for i in range(s.tz):
        total = jnp.zeros((s.V, s.tile), F32)
        for j in range(s.ty):
            spread = jnp.where(lane == (j * s.nx + gx) * s.tx + x // long, 1.0 / long, 0.0)
            total = total + dot(by_vector[i * s.ty + j], spread, precision=lax.Precision.HIGHEST)
        total = total.astype(BF16)
        piece[i * s.V : (i + 1) * s.V, :] = total
        if s.ride:
            for edge in edges:
                at = s.rows + 2 * s.avg + i * s.V
                edge[at : at + s.V, :] = total


def x_weights(s, fine, coarse):
    gx = lax.axis_index("gx")

    def rows(place, count):
        col = iota((count, s.X), 1)
        a = lookup(place - col + R, fine, 2)
        b = 0.5 * lookup((place + E) // 2 - col // 2, coarse, 2)
        return wide([a, b])

    half = s.V // 2
    own = rows(iota((s.X, s.X), 0), s.X).astype(BF16)
    sides = []
    for kind in s.kx:
        c = iota((E, s.X), 0)
        place = jnp.where(upper(gx, kind), s.X + c, c - E)
        place = jnp.where(partner_missing(gx, s.nx, kind), -4 * s.X, place)
        sides.append(jnp.concatenate([rows(place, E)] * half, axis=0).astype(BF16))
    if len(sides) < 2:
        sides += [jnp.zeros((half * E, 2 * s.X), BF16)] * (2 - len(sides))
    return [jnp.concatenate([own] + order, axis=0) for order in (sides, sides[::-1])]


def pick_y(s, up, fine):
    if fine:
        r, c = iota((s.yf, s.rows), 0), iota((s.yf, s.rows), 1)
        y0 = jnp.where(up, s.Y - R, 0)
        return one((c // s.Y == r // R) & (c % s.Y == y0 + r % R))
    r, c = iota((s.yc, s.rows), 0), iota((s.yc, s.rows), 1)
    c0 = jnp.where(up, s.Y // 2 - R, 0)
    return one((c // s.Y // 2 == r // R) & (c % s.Y // 2 == c0 + r % R), 0.25)


def pick_zy(s, up, fine):
    half = s.Y // 2
    if fine:
        r, c = iota((s.zyf, s.raw), 0), iota((s.zyf, s.raw), 1)
        y0 = jnp.where(up, s.Y - R, 0)
        return one((c // s.Y == r // R) & (c % s.Y == y0 + r % R))
    r, c = iota((s.zyc, s.face), 0), iota((s.zyc, s.face), 1)
    q, y = r // R, r % R + jnp.where(up, half - R, 0)
    near = (c < s.raw) & (c // s.Y // 2 == q) & (c % s.Y // 2 == y)
    b = c - s.raw
    far = (c >= s.raw) & (b // half + R // 2 == q) & (b % half == y)
    return jnp.where(near, 0.25, jnp.where(far, 1.0, 0.0)).astype(BF16)


def xpass(s, weights, data, halos, v):
    group = iota((1, s.V * E), 1) // E
    mixed = jnp.zeros((data.shape[0], s.V * E), BF16)
    for i, halo in enumerate(halos):
        mixed = jnp.where(group == lane_group(s, i, v), halo, mixed)
    return dot(wide([data, mixed]), weights[v // (s.V // 2)]).astype(BF16)


def lane_group(s, place, v):
    return (v + place * (s.V // 2)) % s.V


def own_kernel(s, weights, field, *refs):
    n = len(s.kx)
    halos, (own, *packs) = [h[: s.rows, :] for h in refs[:n]], refs[n:]
    for v in range(s.V):
        at = slice(v * s.X, (v + 1) * s.X)
        passed = xpass(s, weights, field[v].reshape(s.rows, s.X), halos, v)
        own[: s.rows, at] = passed[:, : s.X]
        own[s.rows :, at] = passed[:, s.X :]
    gy = lax.axis_index("gy")
    for kind, pack in zip(s.ky, packs):
        up = upper(gy, kind)
        pack[: s.yf, :] = dot(pick_y(s, up, True), own[: s.rows, :]).astype(BF16)
        pack[s.yf :, :] = dot(pick_y(s, up, False), own[s.rows :, :]).astype(BF16)


def sides_kernel(s, weights, *refs):
    m = len(s.kz)
    faces, corners, refs = refs[:m], refs[m : 2 * m], refs[2 * m :]
    sides, packs = refs[:m], refs[m:]
    halos = [
        jnp.concatenate([c[i * s.face : (i + 1) * s.face, :] for c in corners], axis=0)
        for i in range(len(s.kx))
    ]
    for v in range(s.V):
        at = slice(v * s.X, (v + 1) * s.X)
        data = jnp.concatenate([f[v] for f in faces], axis=0)
        passed = xpass(s, weights, data, halos, v)
        for i, side in enumerate(sides):
            base = i * s.face
            side[: s.raw, at] = passed[base : base + s.raw, : s.X]
            side[s.raw :, at] = passed[base : base + s.face, s.X :]
    gy = lax.axis_index("gy")
    for kind, pack in zip(s.ky, packs):
        up = upper(gy, kind)
        at = 0
        for side in sides:
            pack[at : at + s.zyf, :] = dot(pick_zy(s, up, True), side[: s.raw, :]).astype(BF16)
            at += s.zyf
            pack[at : at + s.zyc, :] = dot(pick_zy(s, up, False), side[s.raw :, :]).astype(BF16)
            at += s.zyc


def yz_weights(s, fine, coarse):
    gy, gz = lax.axis_index("gy"), lax.axis_index("gz")
    half, deep = s.Y // 2, s.Z // 2

    def block(taps, z, y, div, scale=None):
        count = z.shape[1]
        a = lookup(z - iota((s.Z, count), 0) // div + R, taps, 0)
        b = lookup(y - iota((s.Y, count), 0) // div + R, taps, 1)
        if scale is not None:
            b = b * scale
        both = a.reshape(s.Z, 1, count) * b.reshape(1, s.Y, count)
        return both.reshape(s.rows, count).astype(BF16)

    c = iota((1, s.rows), 1)
    first = [
        block(fine, c // s.Y, c % s.Y, 1),
        block(coarse, c // s.Y // 2, c % s.Y // 2, 2, 0.25),
    ]
    second = []

    def zplace(kind, z):
        return jnp.where(partner_missing(gz, s.nz, kind), -4 * s.Z, z)

    for kind in s.ky:
        up = upper(gy, kind)
        c = iota((1, s.yf), 1)
        second.append(block(fine, c // R, c % R + jnp.where(up, s.Y, -R), 1))
        c = iota((1, s.yc), 1)
        second.append(block(coarse, c // R, c % R + jnp.where(up, half, -R), 2))
    for kind in s.kz:
        up = upper(gz, kind)
        c = iota((1, s.raw), 1)
        second.append(block(fine, zplace(kind, c // s.Y + jnp.where(up, s.Z, -R)), c % s.Y, 1))
        c = iota((1, s.face), 1)
        b = c - s.raw
        near = c // s.Y // 2 + jnp.where(up, deep, -R // 2)
        far = b // half + jnp.where(up, deep + R // 2, -R)
        z = zplace(kind, jnp.where(c < s.raw, near, far))
        y = jnp.where(c < s.raw, c % s.Y // 2, b % half)
        second.append(block(coarse, z, y, 2, jnp.where(c < s.raw, 0.25, 1.0)))
    for kind in s.ky:
        up = upper(gy, kind)
        fy, cy = jnp.where(up, s.Y, -R), jnp.where(up, half, -R)
        for zkind in s.kz:
            zup = upper(gz, zkind)
            c = iota((1, s.zyf), 1)
            z = zplace(zkind, c // R + jnp.where(zup, s.Z, -R))
            second.append(block(fine, z, c % R + fy, 1))
            c = iota((1, s.zyc), 1)
            q = c // R
            near = q + jnp.where(zup, deep, -R // 2)
            far = q - R // 2 + jnp.where(zup, deep + R // 2, -R)
            z = zplace(zkind, jnp.where(q < R // 2, near, far))
            second.append(block(coarse, z, c % R + cy, 2))
    r, c = iota((s.rows, s.top), 0), iota((s.rows, s.top), 1)
    z, y = r // s.Y // (s.Z // s.tz), r % s.Y // (s.Y // s.ty)
    second.append(one(c // s.tx == z * s.ty + y))
    return first, second


def top_product(s, kernel, parts, total):
    for z, y, part in parts:
        for i in range(s.tz):
            q = pl.multiple_of(((z * s.tz + i) * s.ny + y) * s.tile, s.tile)
            rows = part(slice(i * s.V, (i + 1) * s.V), i)
            total = total + dot(kernel[:, pl.ds(q, s.tile)], rows, ((1,), (1,)))
    return total


def weights_kernel(s, fine, coarse, x, now, later):
    for i, block in enumerate(x_weights(s, fine, coarse)):
        x[i] = block
    first, second = yz_weights(s, fine, coarse)
    for ref, blocks in ((now, first), (later, second)):
        at = 0
        for block in blocks:
            ref[:, at : at + block.shape[1]] = block
            at += block.shape[1]


def partial_kernel(s, now, own, total):
    step = min(s.lanes, 4 * s.X)
    for at in range(0, s.lanes, step):
        cols = slice(at, at + step)
        total[:, cols] = dot(now[...], own[:, cols])


def final_kernel(s, *refs):
    m, k = len(s.kz), len(s.ky)
    partial, later, *refs = refs
    ends, refs = refs[:k], refs[k:]
    sides, refs = refs[:m], refs[m:]
    packs, refs = refs[:k], refs[k:]
    known, kernel, out, held, sems = refs
    gy, gz = lax.axis_index("gy"), lax.axis_index("gz")
    parts = [
        (slot(z, gz, s.nz), slot(y, gy, s.ny), lambda at, i, y=y, z=z: known[y, z, at, :])
        for y in range(s.ny)
        for z in range(s.nz)
    ]
    total = top_product(s, kernel, parts, jnp.zeros((s.top, s.V), F32))
    r, c = iota((s.top, s.X), 0), iota((s.top, s.X), 1)
    spread = c // (s.X // s.tx) == r % s.tx
    chunk = s.V // s.chunks
    copies = []
    pair = 2 if chunk % 2 == 0 else 1
    for v in range(0, s.V, pair):
        cols = slice(v * s.X, (v + pair) * s.X)
        lines = [jnp.broadcast_to(total[:, v + i : v + i + 1], (s.top, s.X)) for i in range(pair)]
        top = wide([jnp.where(spread, line, 0.0).astype(BF16) for line in lines])
        parts = [x[:, cols] for x in (*ends, *sides)]
        parts += [x[:, cols] for x in packs] + [top]
        result = (dot(later[...], jnp.concatenate(parts, axis=0)) + partial[:, cols]).astype(BF16)
        for i in range(pair):
            held[v + i] = result[:, i * s.X : (i + 1) * s.X].reshape(s.Z, s.Y, s.X)
        if (v + pair) % chunk == 0:
            at = pl.ds(v + pair - chunk, chunk)
            copies.append(pltpu.make_async_copy(held.at[at], out.at[at], sems.at[v // chunk]))
            copies[-1].start()
    for copy in copies:
        copy.wait()


def doubling(count):
    return count & (count - 1) == 0


def slot(place, me, count):
    return place ^ me if doubling(count) else place


def gather(a, axis, count, join):
    if not doubling(count):
        return join(list(lax.all_gather(a, axis)))
    step = 1
    while step < count:
        a = join([a, lax.ppermute(a, axis, [(i, i ^ step) for i in range(count)])])
        step *= 2
    return a


def shape(*dims):
    return jax.ShapeDtypeStruct(dims, BF16)


def bind(body, s):
    def kernel(*refs):
        body(s, *refs)

    kernel.__name__ = body.__name__
    return kernel


def shards(sizes, field, fine_taps, coarse_taps, top_kernel):
    s = Sizes(field.shape, top_kernel.shape[:3], sizes)
    n, m, k = len(s.kx), len(s.kz), len(s.ky)

    def run(body, arrays, outs, scalars=0, scratch=(), flops=0, far=(), far_out=False):
        specs = [vmem()] * len(arrays)
        for i in range(scalars):
            specs[i] = smem()
        for i in far:
            specs[i] = pl.BlockSpec(memory_space=pltpu.HBM)
        call = pl.pallas_call(
            bind(body, s),
            out_shape=outs,
            in_specs=specs,
            out_specs=[pl.BlockSpec(memory_space=pltpu.HBM) if far_out else vmem()] * len(outs),
            scratch_shapes=scratch,
            compiler_params=pltpu.CompilerParams(vmem_limit_bytes=24 << 20),
            cost_estimate=pl.CostEstimate(flops=flops, bytes_accessed=1 << 20, transcendentals=0),
        )
        return list(call(*arrays))

    def swap(arrays, axis, count, which, ring=False):
        return [lax.ppermute(a, axis, swaps(count, kind, ring)) for a, kind in zip(arrays, which)]

    buffers = [pltpu.VMEM(field.shape, BF16), pltpu.SemaphoreType.DMA((s.chunks,))]
    top = shape(s.tz * s.V, s.tile)
    outs = [shape(s.V, s.face, s.X)] * m + [shape(s.edge, s.V * E)] * n + [top]
    *faces, field = run(
        front_kernel,
        [pltpu.with_memory_space_constraint(field, pltpu.HBM)],
        outs + [shape(*field.shape)],
        scratch=[pltpu.SemaphoreType.DMA],
        far=(0,),
    )
    faces, edges, piece = faces[:m], faces[m : m + n], faces[-1]
    halos = swap(edges, "gx", s.nx, s.kx, s.ride)
    faces = swap(faces, "gz", s.nz, s.kz)
    corner = [shape(s.corner, s.V * E)] * m
    stack = lambda parts: jnp.concatenate(parts, axis=0)
    if s.ride:
        across = lax.ppermute(piece, "gx", [(i, i ^ 2) for i in range(s.nx)])
        *corners, known = run(corners_kernel, halos + [piece, across], corner + [top])
    else:
        corners = run(corners_kernel, halos, corner)
    corners = swap(corners, "gz", s.nz, s.kz, s.ride)
    if s.ride:
        across = lax.ppermute(known, "gz", [(i, i ^ 2) for i in range(s.nz)])
        near, far = [c[n * s.face :] for c in corners]
        known = jnp.stack([known, near, across, far])
    else:
        known = gather(gather(piece, "gx", s.nx, sum)[None], "gz", s.nz, stack)
    x_depth = s.X + s.V * E
    later = k * (s.yf + s.yc) + m * s.gz + k * s.ypack + s.top
    weights, w_now, w_later = run(
        weights_kernel,
        [pltpu.with_memory_space_constraint(a, pltpu.HBM) for a in (fine_taps, coarse_taps)],
        [
            shape(2, x_depth, 2 * s.X),
            shape(s.rows, 2 * s.rows),
            shape(s.rows, later),
        ],
        scalars=2,
    )
    own, *ends = run(
        own_kernel,
        [weights, field] + halos,
        [shape(2 * s.rows, s.lanes)] + [shape(s.yf + s.yc, s.lanes)] * k,
        flops=4 * s.rows * s.V * x_depth * s.X,
    )
    ends = swap(ends, "gy", s.ny, s.ky)
    rest = run(
        sides_kernel,
        [weights] + faces + corners,
        [shape(s.gz, s.lanes)] * m + [shape(s.ypack, s.lanes)] * k,
    )
    sides, packs = rest[:m], rest[m:]
    packs = swap(packs, "gy", s.ny, s.ky)
    partial = run(
        partial_kernel,
        [w_now, own],
        [jax.ShapeDtypeStruct((s.rows, s.lanes), F32)],
        flops=4 * s.rows * s.rows * s.lanes,
    )[0]
    known = gather(known[None], "gy", s.ny, stack)
    kernel_rows = top_kernel.reshape(s.top, top_kernel.shape[3])
    return run(
        final_kernel,
        [partial, w_later] + ends + sides + packs + [known, kernel_rows],
        [shape(*field.shape)],
        scratch=buffers,
        far_out=True,
    )[0]


def solution(mesh):
    sizes = tuple(mesh.shape[name] for name in ("gx", "gy", "gz"))

    def body(*args):
        return shards(sizes, *args)

    return jax.shard_map(
        body,
        mesh=mesh,
        in_specs=(P(None, "gz", "gy", "gx"), P(), P(), P("gz", "gy", "gx", None)),
        out_specs=P(None, "gz", "gy", "gx"),
        check_vma=False,
    )
```

```python
import jax
import jax.numpy as jnp
from jax import lax
from jax.experimental import pallas as pl
from jax.experimental.pallas import tpu as pltpu
from jax.sharding import PartitionSpec as P


F32 = jnp.float32
BF16 = jnp.bfloat16
R = 4
E = 2 * R


def swaps(count, kind, ring=False):
    pairs = []
    for i in range(kind, count - 1, 2):
        pairs += [(i, i + 1), (i + 1, i)]
    if ring and kind == 1 and pairs and count % 2 == 0:
        pairs += [(0, count - 1), (count - 1, 0)]
    return pairs


def partner_missing(index, count, kind):
    at = index + jnp.where(upper(index, kind), 1, -1)
    return (at < 0) | (at >= count)


def kinds(count):
    return [k for k in (0, 1) if swaps(count, k)]


def upper(index, kind):
    return lax.rem(index + kind, 2) == 0


def iota(shape, dim):
    return lax.broadcasted_iota(jnp.int32, shape, dim)


def dot(a, b, dims=((1,), (0,)), precision=None):
    return lax.dot_general(a, b, (dims, ((), ())), precision=precision, preferred_element_type=F32)


def lookup(offset, taps, row):
    total = jnp.zeros(offset.shape, F32)
    for k in range(2 * R + 1):
        total = jnp.where(offset == k, taps[row, k], total)
    return total


def one(condition, value=1.0):
    return jnp.where(condition, value, 0.0).astype(BF16)


def wide(parts):
    return jnp.concatenate(parts, axis=1)


class Sizes:
    def __init__(self, shape, top_shape, mesh_sizes):
        self.V, self.Z, self.Y, self.X = shape
        self.nx, self.ny, self.nz = mesh_sizes
        self.rows = self.Z * self.Y
        self.lanes = self.V * self.X
        self.raw = R * self.Y
        self.avg = (R // 2) * (self.Y // 2)
        self.face = self.raw + self.avg
        self.kx, self.ky, self.kz = kinds(self.nx), kinds(self.ny), kinds(self.nz)
        self.yf, self.yc = self.Z * R, (self.Z // 2) * R
        self.zyf, self.zyc = R * R, R * R
        self.tz, self.ty, self.tx = top_shape
        self.top = self.tz * self.ty * self.tx
        self.gz = self.raw + self.face
        self.tile = self.ty * self.tx * self.nx
        self.ride = self.nx == 4 and self.nz == 4 and self.tile == self.V * E
        self.edge = self.rows + 2 * self.avg + (self.tz * self.V if self.ride else 0)
        self.ypack = len(self.kz) * (self.zyf + self.zyc)
        self.chunks = 4 if self.V % 4 == 0 else 1
        self.corner = len(self.kx) * self.face + (self.tz * self.V if self.ride else 0)


def smem():
    return pl.BlockSpec(memory_space=pltpu.SMEM)


def vmem():
    return pl.BlockSpec(memory_space=pltpu.VMEM)


def corners_kernel(s, *refs):
    me = lax.axis_index("gz")
    n = len(s.kx)
    halos, refs = refs[:n], refs[n:]
    if s.ride:
        piece, across, *outs, known = refs
        total = piece[...].astype(F32) + across[...].astype(F32)
        for halo in halos:
            total = total + halo[s.rows + 2 * s.avg :, :].astype(F32)
        known[...] = total.astype(BF16)
    else:
        outs = refs
    for kind, out in zip(s.kz, outs):
        up = upper(me, kind)
        start = pl.multiple_of(jnp.where(up, s.rows - s.raw, 0), 16)
        mean = pl.multiple_of(jnp.where(up, s.rows + s.avg, s.rows), 16)
        for i, halo in enumerate(halos):
            at = i * s.face
            out[at : at + s.raw, :] = halo[pl.ds(start, s.raw), :]
            out[at + s.raw : at + s.face, :] = halo[pl.ds(mean, s.avg), :]
        if s.ride:
            out[n * s.face :, :] = total.astype(BF16)


def front_kernel(s, field, fine_far, coarse_far, *refs):
    gx = lax.axis_index("gx")
    n, m = len(s.kx), len(s.kz)
    faces, edges, refs = refs[:m], refs[m : m + n], refs[m + n :]
    piece, weights, held, fine, coarse, found, sems = refs
    taps = [
        pltpu.make_async_copy(fine_far, fine, sems.at[s.chunks]),
        pltpu.make_async_copy(coarse_far, coarse, sems.at[s.chunks + 1]),
    ]
    chunk = s.V // s.chunks
    copies = []
    for i in range(s.chunks):
        at = pl.ds(i * chunk, chunk)
        copies.append(pltpu.make_async_copy(field.at[at], held.at[at], sems.at[i]))
    for each in taps + copies:
        each.start()
    half = s.Y // 2
    deep, tall, long = s.Z // s.tz, s.Y // s.ty, s.X // s.tx
    x, lane = iota((s.X, s.V * E), 0), iota((s.X, s.V * E), 1)
    picks = [one(x - jnp.where(upper(gx, kind), s.X - E, 0) == lane % E) for kind in s.kx]
    group = iota((1, s.V * E), 1) // E
    by_v = [
        wide([jnp.where(group == lane_group(s, j, v), p, jnp.zeros_like(p)) for j, p in enumerate(picks)])
        for v in range(s.V)
    ]
    sub = iota((s.V, s.X), 0)
    gz = lax.axis_index("gz")
    row, col = iota((s.avg, s.raw), 0), iota((s.avg, s.raw), 1)
    mean = one((col // s.Y // 2 == row // half) & (col % s.Y // 2 == row % half), 0.25)
    for each in taps:
        each.wait()
    for i, block in enumerate(x_weights(s, fine, coarse)):
        weights[i] = block
    by_vector = [jnp.zeros((s.V, s.X), F32) for _ in range(s.tz * s.ty)]
    for part, copy in enumerate(copies):
        vectors = range(part * chunk, (part + 1) * chunk)
        copy.wait()
        data = wide([held[v].reshape(s.rows, s.X) for v in vectors])
        more = dot(data, jnp.concatenate([by_v[v] for v in vectors], axis=0))
        found[...] = more if part == 0 else found[...] + more
        for kind, out in zip(s.kz, faces):
            up = upper(gz, kind)
            start = jnp.where(up, s.Z - R, 0)
            further = jnp.where(up, s.Z - E, R)
            for v in vectors:
                out[v, : s.raw, :] = held[v, pl.ds(start, R)].reshape(s.raw, s.X)
            data = wide([held[v, pl.ds(further, R)].reshape(s.raw, s.X) for v in vectors])
            means = dot(mean, data).astype(BF16)
            for v in vectors:
                at = v % chunk * s.X
                out[v, s.raw :, :] = means[:, at : at + s.X]
        for v in vectors:
            for i in range(s.tz):
                layers = held[v, i * deep].astype(F32)
                for z in range(i * deep + 1, (i + 1) * deep):
                    layers = layers + held[v, z].astype(F32)
                for j in range(s.ty):
                    line = jnp.sum(layers[j * tall : (j + 1) * tall], axis=0, keepdims=True)
                    line = jnp.broadcast_to(line * (1.0 / (deep * tall)), (s.V, s.X))
                    by_vector[i * s.ty + j] = jnp.where(sub == v, line, by_vector[i * s.ty + j])
    r, c = iota((2 * s.avg, s.rows), 0), iota((2 * s.avg, s.rows), 1)
    layer = r // half * 2 + jnp.where(r < s.avg, R, s.Z - E - R)
    mean = one((c // s.Y // 2 * 2 == layer) & (c % s.Y // 2 == r % half), 0.25)
    for j in range(n):
        edge = found[:, j * s.V * E : (j + 1) * s.V * E].astype(BF16)
        edges[j][: s.rows, :] = edge
        edges[j][s.rows : s.rows + 2 * s.avg, :] = dot(mean, edge).astype(BF16)
    x, lane = iota((s.X, s.tile), 0), iota((s.X, s.tile), 1)
    for i in range(s.tz):
        total = jnp.zeros((s.V, s.tile), F32)
        for j in range(s.ty):
            spread = jnp.where(lane == (j * s.nx + gx) * s.tx + x // long, 1.0 / long, 0.0)
            total = total + dot(by_vector[i * s.ty + j], spread, precision=lax.Precision.HIGHEST)
        total = total.astype(BF16)
        piece[i * s.V : (i + 1) * s.V, :] = total
        if s.ride:
            for edge in edges:
                at = s.rows + 2 * s.avg + i * s.V
                edge[at : at + s.V, :] = total


def x_weights(s, fine, coarse):
    gx = lax.axis_index("gx")

    def rows(place, count):
        col = iota((count, s.X), 1)
        a = lookup(place - col + R, fine, 2)
        b = 0.5 * lookup((place + E) // 2 - col // 2, coarse, 2)
        return wide([a, b])

    half = s.V // 2
    own = rows(iota((s.X, s.X), 0), s.X).astype(BF16)
    sides = []
    for kind in s.kx:
        c = iota((E, s.X), 0)
        place = jnp.where(upper(gx, kind), s.X + c, c - E)
        place = jnp.where(partner_missing(gx, s.nx, kind), -4 * s.X, place)
        sides.append(jnp.concatenate([rows(place, E)] * half, axis=0).astype(BF16))
    if len(sides) < 2:
        sides += [jnp.zeros((half * E, 2 * s.X), BF16)] * (2 - len(sides))
    return [jnp.concatenate([own] + order, axis=0) for order in (sides, sides[::-1])]


def pick_y(s, up, fine):
    if fine:
        r, c = iota((s.yf, s.rows), 0), iota((s.yf, s.rows), 1)
        y0 = jnp.where(up, s.Y - R, 0)
        return one((c // s.Y == r // R) & (c % s.Y == y0 + r % R))
    r, c = iota((s.yc, s.rows), 0), iota((s.yc, s.rows), 1)
    c0 = jnp.where(up, s.Y // 2 - R, 0)
    return one((c // s.Y // 2 == r // R) & (c % s.Y // 2 == c0 + r % R), 0.25)


def pick_zy(s, up, fine):
    half = s.Y // 2
    if fine:
        r, c = iota((s.zyf, s.raw), 0), iota((s.zyf, s.raw), 1)
        y0 = jnp.where(up, s.Y - R, 0)
        return one((c // s.Y == r // R) & (c % s.Y == y0 + r % R))
    r, c = iota((s.zyc, s.face), 0), iota((s.zyc, s.face), 1)
    q, y = r // R, r % R + jnp.where(up, half - R, 0)
    near = (c < s.raw) & (c // s.Y // 2 == q) & (c % s.Y // 2 == y)
    b = c - s.raw
    far = (c >= s.raw) & (b // half + R // 2 == q) & (b % half == y)
    return jnp.where(near, 0.25, jnp.where(far, 1.0, 0.0)).astype(BF16)


def xpass(s, weights, data, halos, v):
    group = iota((1, s.V * E), 1) // E
    mixed = jnp.zeros((data.shape[0], s.V * E), BF16)
    for i, halo in enumerate(halos):
        mixed = jnp.where(group == lane_group(s, i, v), halo, mixed)
    return dot(wide([data, mixed]), weights[v // (s.V // 2)]).astype(BF16)


def lane_group(s, place, v):
    return (v + place * (s.V // 2)) % s.V


def own_kernel(s, weights, field, *refs):
    n = len(s.kx)
    halos, (own, *packs) = [h[: s.rows, :] for h in refs[:n]], refs[n:]
    for v in range(s.V):
        at = slice(v * s.X, (v + 1) * s.X)
        passed = xpass(s, weights, field[v].reshape(s.rows, s.X), halos, v)
        own[: s.rows, at] = passed[:, : s.X]
        own[s.rows :, at] = passed[:, s.X :]
    gy = lax.axis_index("gy")
    for kind, pack in zip(s.ky, packs):
        up = upper(gy, kind)
        pack[: s.yf, :] = dot(pick_y(s, up, True), own[: s.rows, :]).astype(BF16)
        pack[s.yf :, :] = dot(pick_y(s, up, False), own[s.rows :, :]).astype(BF16)


def sides_kernel(s, weights, *refs):
    m = len(s.kz)
    faces, corners, refs = refs[:m], refs[m : 2 * m], refs[2 * m :]
    sides, packs = refs[:m], refs[m:]
    halos = [
        jnp.concatenate([c[i * s.face : (i + 1) * s.face, :] for c in corners], axis=0)
        for i in range(len(s.kx))
    ]
    for v in range(s.V):
        at = slice(v * s.X, (v + 1) * s.X)
        data = jnp.concatenate([f[v] for f in faces], axis=0)
        passed = xpass(s, weights, data, halos, v)
        for i, side in enumerate(sides):
            base = i * s.face
            side[: s.raw, at] = passed[base : base + s.raw, : s.X]
            side[s.raw :, at] = passed[base : base + s.face, s.X :]
    gy = lax.axis_index("gy")
    for kind, pack in zip(s.ky, packs):
        up = upper(gy, kind)
        at = 0
        for side in sides:
            pack[at : at + s.zyf, :] = dot(pick_zy(s, up, True), side[: s.raw, :]).astype(BF16)
            at += s.zyf
            pack[at : at + s.zyc, :] = dot(pick_zy(s, up, False), side[s.raw :, :]).astype(BF16)
            at += s.zyc


def yz_weights(s, fine, coarse):
    gy, gz = lax.axis_index("gy"), lax.axis_index("gz")
    half, deep = s.Y // 2, s.Z // 2

    def block(taps, z, y, div, scale=None):
        count = z.shape[1]
        a = lookup(z - iota((s.Z, count), 0) // div + R, taps, 0)
        b = lookup(y - iota((s.Y, count), 0) // div + R, taps, 1)
        if scale is not None:
            b = b * scale
        both = a.reshape(s.Z, 1, count) * b.reshape(1, s.Y, count)
        return both.reshape(s.rows, count).astype(BF16)

    c = iota((1, s.rows), 1)
    first = [
        block(fine, c // s.Y, c % s.Y, 1),
        block(coarse, c // s.Y // 2, c % s.Y // 2, 2, 0.25),
    ]
    second = []

    def zplace(kind, z):
        return jnp.where(partner_missing(gz, s.nz, kind), -4 * s.Z, z)

    for kind in s.ky:
        up = upper(gy, kind)
        c = iota((1, s.yf), 1)
        second.append(block(fine, c // R, c % R + jnp.where(up, s.Y, -R), 1))
        c = iota((1, s.yc), 1)
        second.append(block(coarse, c // R, c % R + jnp.where(up, half, -R), 2))
    for kind in s.kz:
        up = upper(gz, kind)
        c = iota((1, s.raw), 1)
        second.append(block(fine, zplace(kind, c // s.Y + jnp.where(up, s.Z, -R)), c % s.Y, 1))
        c = iota((1, s.face), 1)
        b = c - s.raw
        near = c // s.Y // 2 + jnp.where(up, deep, -R // 2)
        far = b // half + jnp.where(up, deep + R // 2, -R)
        z = zplace(kind, jnp.where(c < s.raw, near, far))
        y = jnp.where(c < s.raw, c % s.Y // 2, b % half)
        second.append(block(coarse, z, y, 2, jnp.where(c < s.raw, 0.25, 1.0)))
    for kind in s.ky:
        up = upper(gy, kind)
        fy, cy = jnp.where(up, s.Y, -R), jnp.where(up, half, -R)
        for zkind in s.kz:
            zup = upper(gz, zkind)
            c = iota((1, s.zyf), 1)
            z = zplace(zkind, c // R + jnp.where(zup, s.Z, -R))
            second.append(block(fine, z, c % R + fy, 1))
            c = iota((1, s.zyc), 1)
            q = c // R
            near = q + jnp.where(zup, deep, -R // 2)
            far = q - R // 2 + jnp.where(zup, deep + R // 2, -R)
            z = zplace(zkind, jnp.where(q < R // 2, near, far))
            second.append(block(coarse, z, c % R + cy, 2))
    r, c = iota((s.rows, s.top), 0), iota((s.rows, s.top), 1)
    z, y = r // s.Y // (s.Z // s.tz), r % s.Y // (s.Y // s.ty)
    second.append(one(c // s.tx == z * s.ty + y))
    return first, second


def top_product(s, kernel, parts, total):
    for z, y, part in parts:
        for i in range(s.tz):
            q = pl.multiple_of(((z * s.tz + i) * s.ny + y) * s.tile, s.tile)
            rows = part(slice(i * s.V, (i + 1) * s.V), i)
            total = total + dot(kernel[:, pl.ds(q, s.tile)], rows, ((1,), (1,)))
    return total


def weights_kernel(s, fine, coarse, now, later):
    first, second = yz_weights(s, fine, coarse)
    for ref, blocks in ((now, first), (later, second)):
        at = 0
        for block in blocks:
            ref[:, at : at + block.shape[1]] = block
            at += block.shape[1]


def partial_kernel(s, now, own, total):
    step = min(s.lanes, 4 * s.X)
    for at in range(0, s.lanes, step):
        cols = slice(at, at + step)
        total[:, cols] = dot(now[...], own[:, cols])


def top_own_kernel(s, known, kernel, total):
    gy, gz = lax.axis_index("gy"), lax.axis_index("gz")
    parts = [(slot(z, gz, s.nz), gy, lambda at, i, z=z: known[z, at, :]) for z in range(s.nz)]
    total[...] = top_product(s, kernel, parts, jnp.zeros((s.top, s.V), F32))


def final_kernel(s, *refs):
    m, k = len(s.kz), len(s.ky)
    partial, later, *refs = refs
    ends, refs = refs[:k], refs[k:]
    sides, refs = refs[:m], refs[m:]
    packs, refs = refs[:k], refs[k:]
    started, known, kernel, out, held, sems = refs
    gy, gz = lax.axis_index("gy"), lax.axis_index("gz")
    parts = [
        (slot(z, gz, s.nz), slot(y, gy, s.ny), lambda at, i, y=y, z=z: known[y, z, at, :])
        for y in range(1 if doubling(s.ny) else 0, s.ny)
        for z in range(s.nz)
    ]
    total = top_product(s, kernel, parts, started[...])
    r, c = iota((s.top, s.X), 0), iota((s.top, s.X), 1)
    spread = c // (s.X // s.tx) == r % s.tx
    chunk = s.V // s.chunks
    copies = []
    pair = 2 if chunk % 2 == 0 else 1
    for v in range(0, s.V, pair):
        cols = slice(v * s.X, (v + pair) * s.X)
        lines = [jnp.broadcast_to(total[:, v + i : v + i + 1], (s.top, s.X)) for i in range(pair)]
        top = wide([jnp.where(spread, line, 0.0).astype(BF16) for line in lines])
        parts = [x[:, cols] for x in (*ends, *sides)]
        parts += [x[:, cols] for x in packs] + [top]
        result = (dot(later[...], jnp.concatenate(parts, axis=0)) + partial[:, cols]).astype(BF16)
        for i in range(pair):
            held[v + i] = result[:, i * s.X : (i + 1) * s.X].reshape(s.Z, s.Y, s.X)
        if (v + pair) % chunk == 0:
            at = pl.ds(v + pair - chunk, chunk)
            copies.append(pltpu.make_async_copy(held.at[at], out.at[at], sems.at[v // chunk]))
            copies[-1].start()
    for copy in copies:
        copy.wait()


def doubling(count):
    return count & (count - 1) == 0


def slot(place, me, count):
    return place ^ me if doubling(count) else place


def gather(a, axis, count, join):
    if not doubling(count):
        return join(list(lax.all_gather(a, axis)))
    step = 1
    while step < count:
        a = join([a, lax.ppermute(a, axis, [(i, i ^ step) for i in range(count)])])
        step *= 2
    return a


def shape(*dims):
    return jax.ShapeDtypeStruct(dims, BF16)


def bind(body, s):
    def kernel(*refs):
        body(s, *refs)

    kernel.__name__ = body.__name__
    return kernel


def shards(sizes, field, fine_taps, coarse_taps, top_kernel):
    s = Sizes(field.shape, top_kernel.shape[:3], sizes)
    n, m, k = len(s.kx), len(s.kz), len(s.ky)

    def run(body, arrays, outs, scalars=0, scratch=(), flops=0, far=(), far_out=False):
        specs = [vmem()] * len(arrays)
        for i in range(scalars):
            specs[i] = smem()
        for i in far:
            specs[i] = pl.BlockSpec(memory_space=pltpu.HBM)
        call = pl.pallas_call(
            bind(body, s),
            out_shape=outs,
            in_specs=specs,
            out_specs=[pl.BlockSpec(memory_space=pltpu.HBM) if far_out else vmem()] * len(outs),
            scratch_shapes=scratch,
            compiler_params=pltpu.CompilerParams(vmem_limit_bytes=24 << 20),
            cost_estimate=pl.CostEstimate(flops=flops, bytes_accessed=1 << 20, transcendentals=0),
        )
        return list(call(*arrays))

    def swap(arrays, axis, count, which, ring=False):
        moved = []
        for a, kind in zip(arrays, which):
            moved.append(lax.ppermute(a, axis, swaps(count, kind, ring)))
        return moved

    taps = [fine_taps, coarse_taps]
    buffers = [pltpu.VMEM(field.shape, BF16), pltpu.SemaphoreType.DMA((s.chunks,))]
    top = shape(s.tz * s.V, s.tile)
    x_depth = s.X + s.V * E
    outs = [shape(s.V, s.face, s.X)] * m + [shape(s.edge, s.V * E)] * n
    outs += [top, shape(2, x_depth, 2 * s.X), shape(*field.shape)]
    far = [pltpu.with_memory_space_constraint(a, pltpu.HBM) for a in (field, *taps)]
    *faces, piece, weights, field = run(
        front_kernel,
        far,
        outs,
        scratch=[pltpu.SMEM(a.shape, a.dtype) for a in taps]
        + [
            pltpu.VMEM((s.rows, max(n, 1) * s.V * E), F32),
            pltpu.SemaphoreType.DMA((s.chunks + 2,)),
        ],
        far=(0, 1, 2),
    )
    faces, edges = faces[:m], faces[m:]
    halos = swap(edges, "gx", s.nx, s.kx, s.ride)
    faces = swap(faces, "gz", s.nz, s.kz)
    corner = [shape(s.corner, s.V * E)] * m
    stack = lambda parts: jnp.concatenate(parts, axis=0)
    if s.ride:
        across = lax.ppermute(piece, "gx", [(i, i ^ 2) for i in range(s.nx)])
        *corners, known = run(corners_kernel, halos + [piece, across], corner + [top])
    else:
        corners = run(corners_kernel, halos, corner)
    corners = swap(corners, "gz", s.nz, s.kz, s.ride)
    if s.ride:
        across = lax.ppermute(known, "gz", [(i, i ^ 2) for i in range(s.nz)])
        near, far = [c[n * s.face :] for c in corners]
        known = jnp.stack([known, near, across, far])
    else:
        known = gather(gather(piece, "gx", s.nx, sum)[None], "gz", s.nz, stack)
    later = k * (s.yf + s.yc) + m * s.gz + k * s.ypack + s.top
    w_now, w_later = run(
        weights_kernel,
        taps,
        [shape(s.rows, 2 * s.rows), shape(s.rows, later)],
        scalars=2,
        flops=1 << 28,
    )
    own, *ends = run(
        own_kernel,
        [weights, field] + halos,
        [shape(2 * s.rows, s.lanes)] + [shape(s.yf + s.yc, s.lanes)] * k,
        flops=4 * s.rows * s.V * x_depth * s.X,
    )
    ends = swap(ends, "gy", s.ny, s.ky)
    rest = run(
        sides_kernel,
        [weights] + faces + corners,
        [shape(s.gz, s.lanes)] * m + [shape(s.ypack, s.lanes)] * k,
    )
    sides, packs = rest[:m], rest[m:]
    packs = swap(packs, "gy", s.ny, s.ky)
    partial = run(
        partial_kernel,
        [w_now, own],
        [jax.ShapeDtypeStruct((s.rows, s.lanes), F32)],
        flops=4 * s.rows * s.rows * s.lanes,
    )[0]
    kernel_rows = top_kernel.reshape(s.top, top_kernel.shape[3])
    started = jnp.zeros((s.top, s.V), F32)
    if doubling(s.ny):
        started = run(
            top_own_kernel, [known, kernel_rows], [jax.ShapeDtypeStruct((s.top, s.V), F32)]
        )[0]
    known = gather(known[None], "gy", s.ny, stack)
    return run(
        final_kernel,
        [partial, w_later] + ends + sides + packs + [started, known, kernel_rows],
        [shape(*field.shape)],
        scratch=buffers,
        far_out=True,
    )[0]


def solution(mesh):
    sizes = tuple(mesh.shape[name] for name in ("gx", "gy", "gz"))

    def body(*args):
        return shards(sizes, *args)

    return jax.shard_map(
        body,
        mesh=mesh,
        in_specs=(P(None, "gz", "gy", "gx"), P(), P(), P("gz", "gy", "gx", None)),
        out_specs=P(None, "gz", "gy", "gx"),
        check_vma=False,
    )
```

```python
import jax
import jax.numpy as jnp
from jax import lax
from jax.experimental import pallas as pl
from jax.experimental.pallas import tpu as pltpu
from jax.sharding import PartitionSpec as P


F32 = jnp.float32
BF16 = jnp.bfloat16
R = 4
E = 2 * R


def swaps(count, kind, ring=False):
    pairs = []
    for i in range(kind, count - 1, 2):
        pairs += [(i, i + 1), (i + 1, i)]
    if ring and kind == 1 and pairs and count % 2 == 0:
        pairs += [(0, count - 1), (count - 1, 0)]
    return pairs


def partner_missing(index, count, kind):
    at = index + jnp.where(upper(index, kind), 1, -1)
    return (at < 0) | (at >= count)


def kinds(count):
    return [k for k in (0, 1) if swaps(count, k)]


def upper(index, kind):
    return lax.rem(index + kind, 2) == 0


def iota(shape, dim):
    return lax.broadcasted_iota(jnp.int32, shape, dim)


def dot(a, b, dims=((1,), (0,)), precision=None):
    return lax.dot_general(a, b, (dims, ((), ())), precision=precision, preferred_element_type=F32)


def lookup(offset, taps, row):
    total = jnp.zeros(offset.shape, F32)
    for k in range(2 * R + 1):
        total = jnp.where(offset == k, taps[row, k], total)
    return total


def one(condition, value=1.0):
    return jnp.where(condition, value, 0.0).astype(BF16)


def wide(parts):
    return jnp.concatenate(parts, axis=1)


class Sizes:
    def __init__(self, shape, top_shape, mesh_sizes):
        self.V, self.Z, self.Y, self.X = shape
        self.nx, self.ny, self.nz = mesh_sizes
        self.rows = self.Z * self.Y
        self.lanes = self.V * self.X
        self.raw = R * self.Y
        self.avg = (R // 2) * (self.Y // 2)
        self.face = self.raw + self.avg
        self.kx, self.ky, self.kz = kinds(self.nx), kinds(self.ny), kinds(self.nz)
        self.yf, self.yc = self.Z * R, (self.Z // 2) * R
        self.zyf, self.zyc = R * R, R * R
        self.tz, self.ty, self.tx = top_shape
        self.top = self.tz * self.ty * self.tx
        self.gz = self.raw + self.face
        self.sent = self.V * self.raw + self.V // 2 * self.avg
        self.tile = self.ty * self.tx * self.nx
        self.ride = self.nx == 4 and self.nz == 4 and self.tile == self.V * E
        self.edge = self.rows + 2 * self.avg + (self.tz * self.V if self.ride else 0)
        self.ypack = len(self.kz) * (self.zyf + self.zyc)
        self.chunks = 4 if self.V % 4 == 0 else 1
        self.corner = len(self.kx) * self.face + (self.tz * self.V if self.ride else 0)


def smem():
    return pl.BlockSpec(memory_space=pltpu.SMEM)


def vmem():
    return pl.BlockSpec(memory_space=pltpu.VMEM)


def corners_kernel(s, *refs):
    me = lax.axis_index("gz")
    n = len(s.kx)
    halos, refs = refs[:n], refs[n:]
    if s.ride:
        piece, across, *outs, known = refs
        total = piece[...].astype(F32) + across[...].astype(F32)
        for halo in halos:
            total = total + halo[s.rows + 2 * s.avg :, :].astype(F32)
        known[...] = total.astype(BF16)
    else:
        outs = refs
    for kind, out in zip(s.kz, outs):
        up = upper(me, kind)
        start = pl.multiple_of(jnp.where(up, s.rows - s.raw, 0), 16)
        mean = pl.multiple_of(jnp.where(up, s.rows + s.avg, s.rows), 16)
        for i, halo in enumerate(halos):
            at = i * s.face
            out[at : at + s.raw, :] = halo[pl.ds(start, s.raw), :]
            out[at + s.raw : at + s.face, :] = halo[pl.ds(mean, s.avg), :]
        if s.ride:
            out[n * s.face :, :] = total.astype(BF16)


def front_kernel(s, field, fine_far, coarse_far, *refs):
    gx = lax.axis_index("gx")
    n, m = len(s.kx), len(s.kz)
    faces, edges, refs = refs[:m], refs[m : m + n], refs[m + n :]
    piece, weights, held, fine, coarse, found, sems = refs
    taps = [
        pltpu.make_async_copy(fine_far, fine, sems.at[s.chunks]),
        pltpu.make_async_copy(coarse_far, coarse, sems.at[s.chunks + 1]),
    ]
    chunk = s.V // s.chunks
    copies = []
    for i in range(s.chunks):
        at = pl.ds(i * chunk, chunk)
        copies.append(pltpu.make_async_copy(field.at[at], held.at[at], sems.at[i]))
    for each in taps + copies:
        each.start()
    half = s.Y // 2
    deep, tall, long = s.Z // s.tz, s.Y // s.ty, s.X // s.tx
    x, lane = iota((s.X, s.V * E), 0), iota((s.X, s.V * E), 1)
    picks = [one(x - jnp.where(upper(gx, kind), s.X - E, 0) == lane % E) for kind in s.kx]
    group = iota((1, s.V * E), 1) // E
    by_v = [
        wide([jnp.where(group == lane_group(s, j, v), p, jnp.zeros_like(p)) for j, p in enumerate(picks)])
        for v in range(s.V)
    ]
    sub = iota((s.V, s.X), 0)
    gz = lax.axis_index("gz")
    row, col = iota((s.avg, s.raw), 0), iota((s.avg, s.raw), 1)
    mean = one((col // s.Y // 2 == row // half) & (col % s.Y // 2 == row % half), 0.25)
    r, c = iota((2 * s.X, s.X), 0), iota((2 * s.X, s.X), 1)
    halve = one(r // 2 == c, 0.5)
    for each in taps:
        each.wait()
    *blocks, pairs_block = x_weights(s, fine, coarse)
    for i, block in enumerate(blocks):
        weights[i] = block
    weights[2, : s.X, : s.X] = pairs_block
    by_vector = [jnp.zeros((s.V, s.X), F32) for _ in range(s.tz * s.ty)]
    stacked = {kind: [] for kind in s.kz}
    for part, copy in enumerate(copies):
        vectors = range(part * chunk, (part + 1) * chunk)
        copy.wait()
        data = wide([held[v].reshape(s.rows, s.X) for v in vectors])
        more = dot(data, jnp.concatenate([by_v[v] for v in vectors], axis=0))
        found[...] = more if part == 0 else found[...] + more
        for kind, out in zip(s.kz, faces):
            up = upper(gz, kind)
            start = jnp.where(up, s.Z - R, 0)
            further = jnp.where(up, s.Z - E, R)
            for v in vectors:
                at = v * s.raw
                out[at : at + s.raw, :] = held[v, pl.ds(start, R)].reshape(s.raw, s.X)
            data = wide([held[v, pl.ds(further, R)].reshape(s.raw, s.X) for v in vectors])
            means = dot(mean, data).astype(BF16)
            for i in range(0, chunk, 2):
                stacked[kind].append(means[:, i * s.X : (i + 2) * s.X])
        for v in vectors:
            for i in range(s.tz):
                layers = held[v, i * deep].astype(F32)
                for z in range(i * deep + 1, (i + 1) * deep):
                    layers = layers + held[v, z].astype(F32)
                for j in range(s.ty):
                    line = jnp.sum(layers[j * tall : (j + 1) * tall], axis=0, keepdims=True)
                    line = jnp.broadcast_to(line * (1.0 / (deep * tall)), (s.V, s.X))
                    by_vector[i * s.ty + j] = jnp.where(sub == v, line, by_vector[i * s.ty + j])
    if faces:
        means = dot(jnp.concatenate([x for kind in s.kz for x in stacked[kind]], axis=0), halve)
        count = s.V // 2 * s.avg
        for i, out in enumerate(faces):
            out[s.V * s.raw :, :] = means[i * count : (i + 1) * count].astype(BF16)
    r, c = iota((2 * s.avg, s.rows), 0), iota((2 * s.avg, s.rows), 1)
    layer = r // half * 2 + jnp.where(r < s.avg, R, s.Z - E - R)
    mean = one((c // s.Y // 2 * 2 == layer) & (c % s.Y // 2 == r % half), 0.25)
    for j in range(n):
        edge = found[:, j * s.V * E : (j + 1) * s.V * E].astype(BF16)
        edges[j][: s.rows, :] = edge
        edges[j][s.rows : s.rows + 2 * s.avg, :] = dot(mean, edge).astype(BF16)
    x, lane = iota((s.X, s.tile), 0), iota((s.X, s.tile), 1)
    for i in range(s.tz):
        total = jnp.zeros((s.V, s.tile), F32)
        for j in range(s.ty):
            spread = jnp.where(lane == (j * s.nx + gx) * s.tx + x // long, 1.0 / long, 0.0)
            total = total + dot(by_vector[i * s.ty + j], spread, precision=lax.Precision.HIGHEST)
        total = total.astype(BF16)
        piece[i * s.V : (i + 1) * s.V, :] = total
        if s.ride:
            for edge in edges:
                at = s.rows + 2 * s.avg + i * s.V
                edge[at : at + s.V, :] = total


def x_weights(s, fine, coarse):
    gx = lax.axis_index("gx")

    def rows(place, count):
        col = iota((count, s.X), 1)
        a = lookup(place - col + R, fine, 2)
        b = 0.5 * lookup((place + E) // 2 - col // 2, coarse, 2)
        return wide([a, b])

    half = s.V // 2
    own = rows(iota((s.X, s.X), 0), s.X).astype(BF16)
    sides = []
    for kind in s.kx:
        c = iota((E, s.X), 0)
        place = jnp.where(upper(gx, kind), s.X + c, c - E)
        place = jnp.where(partner_missing(gx, s.nx, kind), -4 * s.X, place)
        sides.append(jnp.concatenate([rows(place, E)] * half, axis=0).astype(BF16))
    if len(sides) < 2:
        sides += [jnp.zeros((half * E, 2 * s.X), BF16)] * (2 - len(sides))
    both = [jnp.concatenate([own] + order, axis=0) for order in (sides, sides[::-1])]
    c, col = iota((s.X, s.X), 0) % (s.X // 2), iota((s.X, s.X), 1)
    return both + [lookup(c - col // 2 + R, coarse, 2).astype(BF16)]


def pick_y(s, up, fine):
    if fine:
        r, c = iota((s.yf, s.rows), 0), iota((s.yf, s.rows), 1)
        y0 = jnp.where(up, s.Y - R, 0)
        return one((c // s.Y == r // R) & (c % s.Y == y0 + r % R))
    r, c = iota((s.yc, s.rows), 0), iota((s.yc, s.rows), 1)
    c0 = jnp.where(up, s.Y // 2 - R, 0)
    return one((c // s.Y // 2 == r // R) & (c % s.Y // 2 == c0 + r % R), 0.25)


def pick_zy(s, up, fine):
    half = s.Y // 2
    if fine:
        r, c = iota((s.zyf, s.raw), 0), iota((s.zyf, s.raw), 1)
        y0 = jnp.where(up, s.Y - R, 0)
        return one((c // s.Y == r // R) & (c % s.Y == y0 + r % R))
    r, c = iota((s.zyc, s.face), 0), iota((s.zyc, s.face), 1)
    q, y = r // R, r % R + jnp.where(up, half - R, 0)
    near = (c < s.raw) & (c // s.Y // 2 == q) & (c % s.Y // 2 == y)
    b = c - s.raw
    far = (c >= s.raw) & (b // half + R // 2 == q) & (b % half == y)
    return jnp.where(near, 0.25, jnp.where(far, 1.0, 0.0)).astype(BF16)


def mix(s, halos, v):
    group = iota((1, s.V * E), 1) // E
    mixed = jnp.zeros((halos[0].shape[0] if halos else 0, s.V * E), BF16)
    for i, halo in enumerate(halos):
        mixed = jnp.where(group == lane_group(s, i, v), halo, mixed)
    return mixed


def xpass(s, weights, data, halos, v):
    mixed = mix(s, halos, v) if halos else jnp.zeros((data.shape[0], s.V * E), BF16)
    return dot(wide([data, mixed]), weights[v // (s.V // 2)]).astype(BF16)


def lane_group(s, place, v):
    return (v + place * (s.V // 2)) % s.V


def own_kernel(s, weights, field, *refs):
    n = len(s.kx)
    halos, (own, *packs) = [h[: s.rows, :] for h in refs[:n]], refs[n:]
    for v in range(s.V):
        at = slice(v * s.X, (v + 1) * s.X)
        passed = xpass(s, weights, field[v].reshape(s.rows, s.X), halos, v)
        own[: s.rows, at] = passed[:, : s.X]
        own[s.rows :, at] = passed[:, s.X :]
    gy = lax.axis_index("gy")
    for kind, pack in zip(s.ky, packs):
        up = upper(gy, kind)
        pack[: s.yf, :] = dot(pick_y(s, up, True), own[: s.rows, :]).astype(BF16)
        pack[s.yf :, :] = dot(pick_y(s, up, False), own[s.rows :, :]).astype(BF16)


def sides_kernel(s, weights, *refs):
    m = len(s.kz)
    faces, corners, refs = refs[:m], refs[m : 2 * m], refs[2 * m :]
    sides, packs = refs[:m], refs[m:]
    near, far = [], []
    for i in range(len(s.kx)):
        at = i * s.face
        near.append(jnp.concatenate([c[at : at + s.raw, :] for c in corners], axis=0))
        far.append(jnp.concatenate([c[at + s.raw : at + s.face, :] for c in corners], axis=0))
    for v in range(s.V):
        at = slice(v * s.X, (v + 1) * s.X)
        data = jnp.concatenate([f[v * s.raw : (v + 1) * s.raw, :] for f in faces], axis=0)
        passed = xpass(s, weights, data, near, v)
        for i, side in enumerate(sides):
            rows = slice(i * s.raw, (i + 1) * s.raw)
            side[: s.raw, at] = passed[rows, : s.X]
            side[s.raw : 2 * s.raw, at] = passed[rows, s.X :]
    right = iota((1, s.X), 1) // (s.X // 2)
    half = s.V // 2
    for h in range(2):
        rows = []
        for v in range(h * half, (h + 1) * half):
            at = s.V * s.raw + v // 2 * s.avg
            data = jnp.concatenate([f[at : at + s.avg, :] for f in faces], axis=0)
            data = jnp.where(right == v % 2, data, jnp.zeros_like(data))
            mixed = mix(s, far, v) if far else jnp.zeros_like(data)
            rows.append(wide([data, mixed]))
        w = jnp.concatenate([weights[2, : s.X, : s.X], weights[h, s.X :, s.X :]], axis=0)
        passed = dot(jnp.concatenate(rows, axis=0), w).astype(BF16)
        for v in range(h * half, (h + 1) * half):
            for i, side in enumerate(sides):
                at = ((v % half) * len(faces) + i) * s.avg
                side[2 * s.raw :, v * s.X : (v + 1) * s.X] = passed[at : at + s.avg, :]
    gy = lax.axis_index("gy")
    for kind, pack in zip(s.ky, packs):
        up = upper(gy, kind)
        at = 0
        for side in sides:
            pack[at : at + s.zyf, :] = dot(pick_zy(s, up, True), side[: s.raw, :]).astype(BF16)
            at += s.zyf
            pack[at : at + s.zyc, :] = dot(pick_zy(s, up, False), side[s.raw :, :]).astype(BF16)
            at += s.zyc


def yz_weights(s, fine, coarse):
    gy, gz = lax.axis_index("gy"), lax.axis_index("gz")
    half, deep = s.Y // 2, s.Z // 2

    def block(taps, z, y, div, scale=None):
        count = z.shape[1]
        a = lookup(z - iota((s.Z, count), 0) // div + R, taps, 0)
        b = lookup(y - iota((s.Y, count), 0) // div + R, taps, 1)
        if scale is not None:
            b = b * scale
        both = a.reshape(s.Z, 1, count) * b.reshape(1, s.Y, count)
        return both.reshape(s.rows, count).astype(BF16)

    c = iota((1, s.rows), 1)
    first = [
        block(fine, c // s.Y, c % s.Y, 1),
        block(coarse, c // s.Y // 2, c % s.Y // 2, 2, 0.25),
    ]
    second = []

    def zplace(kind, z):
        return jnp.where(partner_missing(gz, s.nz, kind), -4 * s.Z, z)

    for kind in s.ky:
        up = upper(gy, kind)
        c = iota((1, s.yf), 1)
        second.append(block(fine, c // R, c % R + jnp.where(up, s.Y, -R), 1))
        c = iota((1, s.yc), 1)
        second.append(block(coarse, c // R, c % R + jnp.where(up, half, -R), 2))
    for kind in s.kz:
        up = upper(gz, kind)
        c = iota((1, s.raw), 1)
        second.append(block(fine, zplace(kind, c // s.Y + jnp.where(up, s.Z, -R)), c % s.Y, 1))
        c = iota((1, s.face), 1)
        b = c - s.raw
        near = c // s.Y // 2 + jnp.where(up, deep, -R // 2)
        far = b // half + jnp.where(up, deep + R // 2, -R)
        z = zplace(kind, jnp.where(c < s.raw, near, far))
        y = jnp.where(c < s.raw, c % s.Y // 2, b % half)
        second.append(block(coarse, z, y, 2, jnp.where(c < s.raw, 0.25, 1.0)))
    for kind in s.ky:
        up = upper(gy, kind)
        fy, cy = jnp.where(up, s.Y, -R), jnp.where(up, half, -R)
        for zkind in s.kz:
            zup = upper(gz, zkind)
            c = iota((1, s.zyf), 1)
            z = zplace(zkind, c // R + jnp.where(zup, s.Z, -R))
            second.append(block(fine, z, c % R + fy, 1))
            c = iota((1, s.zyc), 1)
            q = c // R
            near = q + jnp.where(zup, deep, -R // 2)
            far = q - R // 2 + jnp.where(zup, deep + R // 2, -R)
            z = zplace(zkind, jnp.where(q < R // 2, near, far))
            second.append(block(coarse, z, c % R + cy, 2))
    r, c = iota((s.rows, s.top), 0), iota((s.rows, s.top), 1)
    z, y = r // s.Y // (s.Z // s.tz), r % s.Y // (s.Y // s.ty)
    second.append(one(c // s.tx == z * s.ty + y))
    return first, second


def top_product(s, kernel, parts, total):
    for z, y, part in parts:
        for i in range(s.tz):
            q = pl.multiple_of(((z * s.tz + i) * s.ny + y) * s.tile, s.tile)
            rows = part(slice(i * s.V, (i + 1) * s.V), i)
            total = total + dot(kernel[:, pl.ds(q, s.tile)], rows, ((1,), (1,)))
    return total


def weights_kernel(s, fine, coarse, now, later):
    first, second = yz_weights(s, fine, coarse)
    for ref, blocks in ((now, first), (later, second)):
        at = 0
        for block in blocks:
            ref[:, at : at + block.shape[1]] = block
            at += block.shape[1]


def partial_kernel(s, now, own, total):
    step = min(s.lanes, 4 * s.X)
    for at in range(0, s.lanes, step):
        cols = slice(at, at + step)
        total[:, cols] = dot(now[...], own[:, cols])


def top_own_kernel(s, known, kernel, total):
    gy, gz = lax.axis_index("gy"), lax.axis_index("gz")
    parts = [(slot(z, gz, s.nz), gy, lambda at, i, z=z: known[z, at, :]) for z in range(s.nz)]
    total[...] = top_product(s, kernel, parts, jnp.zeros((s.top, s.V), F32))


def final_kernel(s, *refs):
    m, k = len(s.kz), len(s.ky)
    partial, later, *refs = refs
    ends, refs = refs[:k], refs[k:]
    sides, refs = refs[:m], refs[m:]
    packs, refs = refs[:k], refs[k:]
    started, known, kernel, out, held, sems = refs
    gy, gz = lax.axis_index("gy"), lax.axis_index("gz")
    parts = [
        (slot(z, gz, s.nz), slot(y, gy, s.ny), lambda at, i, y=y, z=z: known[y, z, at, :])
        for y in range(1 if doubling(s.ny) else 0, s.ny)
        for z in range(s.nz)
    ]
    total = top_product(s, kernel, parts, started[...])
    r, c = iota((s.top, s.X), 0), iota((s.top, s.X), 1)
    spread = c // (s.X // s.tx) == r % s.tx
    chunk = s.V // s.chunks
    copies = []
    pair = 2 if chunk % 2 == 0 else 1
    for v in range(0, s.V, pair):
        cols = slice(v * s.X, (v + pair) * s.X)
        lines = [jnp.broadcast_to(total[:, v + i : v + i + 1], (s.top, s.X)) for i in range(pair)]
        top = wide([jnp.where(spread, line, 0.0).astype(BF16) for line in lines])
        parts = [x[:, cols] for x in (*ends, *sides)]
        parts += [x[:, cols] for x in packs] + [top]
        result = (dot(later[...], jnp.concatenate(parts, axis=0)) + partial[:, cols]).astype(BF16)
        for i in range(pair):
            held[v + i] = result[:, i * s.X : (i + 1) * s.X].reshape(s.Z, s.Y, s.X)
        if (v + pair) % chunk == 0:
            at = pl.ds(v + pair - chunk, chunk)
            copies.append(pltpu.make_async_copy(held.at[at], out.at[at], sems.at[v // chunk]))
            copies[-1].start()
    for copy in copies:
        copy.wait()


def doubling(count):
    return count & (count - 1) == 0


def slot(place, me, count):
    return place ^ me if doubling(count) else place


def gather(a, axis, count, join):
    if not doubling(count):
        return join(list(lax.all_gather(a, axis)))
    step = 1
    while step < count:
        a = join([a, lax.ppermute(a, axis, [(i, i ^ step) for i in range(count)])])
        step *= 2
    return a


def shape(*dims):
    return jax.ShapeDtypeStruct(dims, BF16)


def bind(body, s):
    def kernel(*refs):
        body(s, *refs)

    kernel.__name__ = body.__name__
    return kernel


def shards(sizes, field, fine_taps, coarse_taps, top_kernel):
    s = Sizes(field.shape, top_kernel.shape[:3], sizes)
    n, m, k = len(s.kx), len(s.kz), len(s.ky)

    def run(body, arrays, outs, scalars=0, scratch=(), flops=0, far=(), far_out=False):
        specs = [vmem()] * len(arrays)
        for i in range(scalars):
            specs[i] = smem()
        for i in far:
            specs[i] = pl.BlockSpec(memory_space=pltpu.HBM)
        call = pl.pallas_call(
            bind(body, s),
            out_shape=outs,
            in_specs=specs,
            out_specs=[pl.BlockSpec(memory_space=pltpu.HBM) if far_out else vmem()] * len(outs),
            scratch_shapes=scratch,
            compiler_params=pltpu.CompilerParams(vmem_limit_bytes=24 << 20),
            cost_estimate=pl.CostEstimate(flops=flops, bytes_accessed=1 << 20, transcendentals=0),
        )
        return list(call(*arrays))

    def swap(arrays, axis, count, which, ring=False):
        moved = []
        for a, kind in zip(arrays, which):
            moved.append(lax.ppermute(a, axis, swaps(count, kind, ring)))
        return moved

    taps = [fine_taps, coarse_taps]
    buffers = [pltpu.VMEM(field.shape, BF16), pltpu.SemaphoreType.DMA((s.chunks,))]
    top = shape(s.tz * s.V, s.tile)
    x_depth = s.X + s.V * E
    outs = [shape(s.sent, s.X)] * m + [shape(s.edge, s.V * E)] * n
    outs += [top, shape(3, x_depth, 2 * s.X), shape(*field.shape)]
    far = [pltpu.with_memory_space_constraint(a, pltpu.HBM) for a in (field, *taps)]
    *faces, piece, weights, field = run(
        front_kernel,
        far,
        outs,
        scratch=[pltpu.SMEM(a.shape, a.dtype) for a in taps]
        + [
            pltpu.VMEM((s.rows, max(n, 1) * s.V * E), F32),
            pltpu.SemaphoreType.DMA((s.chunks + 2,)),
        ],
        far=(0, 1, 2),
    )
    faces, edges = faces[:m], faces[m:]
    halos = swap(edges, "gx", s.nx, s.kx, s.ride)
    faces = swap(faces, "gz", s.nz, s.kz)
    corner = [shape(s.corner, s.V * E)] * m
    stack = lambda parts: jnp.concatenate(parts, axis=0)
    if s.ride:
        across = lax.ppermute(piece, "gx", [(i, i ^ 2) for i in range(s.nx)])
        *corners, known = run(corners_kernel, halos + [piece, across], corner + [top])
    else:
        corners = run(corners_kernel, halos, corner)
    corners = swap(corners, "gz", s.nz, s.kz, s.ride)
    if s.ride:
        across = lax.ppermute(known, "gz", [(i, i ^ 2) for i in range(s.nz)])
        near, far = [c[n * s.face :] for c in corners]
        known = jnp.stack([known, near, across, far])
    else:
        known = gather(gather(piece, "gx", s.nx, sum)[None], "gz", s.nz, stack)
    later = k * (s.yf + s.yc) + m * s.gz + k * s.ypack + s.top
    w_now, w_later = run(
        weights_kernel,
        taps,
        [shape(s.rows, 2 * s.rows), shape(s.rows, later)],
        scalars=2,
        flops=1 << 28,
    )
    own, *ends = run(
        own_kernel,
        [weights, field] + halos,
        [shape(2 * s.rows, s.lanes)] + [shape(s.yf + s.yc, s.lanes)] * k,
        flops=4 * s.rows * s.V * x_depth * s.X,
    )
    ends = swap(ends, "gy", s.ny, s.ky)
    rest = run(
        sides_kernel,
        [weights] + faces + corners,
        [shape(s.gz, s.lanes)] * m + [shape(s.ypack, s.lanes)] * k,
    )
    sides, packs = rest[:m], rest[m:]
    packs = swap(packs, "gy", s.ny, s.ky)
    partial = run(
        partial_kernel,
        [w_now, own],
        [jax.ShapeDtypeStruct((s.rows, s.lanes), F32)],
        flops=4 * s.rows * s.rows * s.lanes,
    )[0]
    kernel_rows = top_kernel.reshape(s.top, top_kernel.shape[3])
    started = jnp.zeros((s.top, s.V), F32)
    if doubling(s.ny):
        started = run(
            top_own_kernel, [known, kernel_rows], [jax.ShapeDtypeStruct((s.top, s.V), F32)]
        )[0]
    known = gather(known[None], "gy", s.ny, stack)
    return run(
        final_kernel,
        [partial, w_later] + ends + sides + packs + [started, known, kernel_rows],
        [shape(*field.shape)],
        scratch=buffers,
        far_out=True,
    )[0]


def solution(mesh):
    sizes = tuple(mesh.shape[name] for name in ("gx", "gy", "gz"))

    def body(*args):
        return shards(sizes, *args)

    return jax.shard_map(
        body,
        mesh=mesh,
        in_specs=(P(None, "gz", "gy", "gx"), P(), P(), P("gz", "gy", "gx", None)),
        out_specs=P(None, "gz", "gy", "gx"),
        check_vma=False,
    )
```

```python
import jax
import jax.numpy as jnp
from jax import lax
from jax.experimental import pallas as pl
from jax.experimental.pallas import tpu as pltpu
from jax.sharding import PartitionSpec as P


F32 = jnp.float32
BF16 = jnp.bfloat16
R = 4
E = 2 * R


def swaps(count, kind, ring=False):
    pairs = []
    for i in range(kind, count - 1, 2):
        pairs += [(i, i + 1), (i + 1, i)]
    if ring and kind == 1 and pairs and count % 2 == 0:
        pairs += [(0, count - 1), (count - 1, 0)]
    return pairs


def partner_missing(index, count, kind):
    at = index + jnp.where(upper(index, kind), 1, -1)
    return (at < 0) | (at >= count)


def kinds(count):
    return [k for k in (0, 1) if swaps(count, k)]


def upper(index, kind):
    return lax.rem(index + kind, 2) == 0


def iota(shape, dim):
    return lax.broadcasted_iota(jnp.int32, shape, dim)


def dot(a, b, dims=((1,), (0,)), precision=None):
    return lax.dot_general(a, b, (dims, ((), ())), precision=precision, preferred_element_type=F32)


def lookup(offset, taps, row):
    total = jnp.zeros(offset.shape, F32)
    for k in range(2 * R + 1):
        total = jnp.where(offset == k, taps[row, k], total)
    return total


def one(condition, value=1.0):
    return jnp.where(condition, value, 0.0).astype(BF16)


def split(a):
    high = a.astype(BF16)
    return high, (a - high.astype(F32)).astype(BF16)


def wide(parts):
    return jnp.concatenate(parts, axis=1)


class Sizes:
    def __init__(self, shape, top_shape, mesh_sizes):
        self.V, self.Z, self.Y, self.X = shape
        self.nx, self.ny, self.nz = mesh_sizes
        self.rows = self.Z * self.Y
        self.lanes = self.V * self.X
        self.raw = R * self.Y
        self.avg = (R // 2) * (self.Y // 2)
        self.face = self.raw + self.avg
        self.kx, self.ky, self.kz = kinds(self.nx), kinds(self.ny), kinds(self.nz)
        self.yf, self.yc = self.Z * R, (self.Z // 2) * R
        self.zyf, self.zyc = R * R, R * R
        self.tz, self.ty, self.tx = top_shape
        self.top = self.tz * self.ty * self.tx
        self.gz = self.raw + self.face
        self.sent = self.V * self.raw + self.V // 2 * self.avg
        self.tile = self.ty * self.tx * self.nx
        self.ride = self.nx == 4 and self.nz == 4 and self.tile == self.V * E
        self.edge = self.rows + 2 * self.avg + (self.tz * self.V if self.ride else 0)
        self.ypack = len(self.kz) * (self.zyf + self.zyc)
        self.chunks = 4 if self.V % 4 == 0 else 1
        self.corner = len(self.kx) * self.face + (self.tz * self.V if self.ride else 0)


def smem():
    return pl.BlockSpec(memory_space=pltpu.SMEM)


def vmem():
    return pl.BlockSpec(memory_space=pltpu.VMEM)


def corners_kernel(s, *refs):
    me = lax.axis_index("gz")
    n = len(s.kx)
    halos, refs = refs[:n], refs[n:]
    if s.ride:
        piece, across, *outs, known = refs
        total = piece[...].astype(F32) + across[...].astype(F32)
        for halo in halos:
            total = total + halo[s.rows + 2 * s.avg :, :].astype(F32)
        known[...] = total.astype(BF16)
    else:
        outs = refs
    for kind, out in zip(s.kz, outs):
        up = upper(me, kind)
        start = pl.multiple_of(jnp.where(up, s.rows - s.raw, 0), 16)
        mean = pl.multiple_of(jnp.where(up, s.rows + s.avg, s.rows), 16)
        for i, halo in enumerate(halos):
            at = i * s.face
            out[at : at + s.raw, :] = halo[pl.ds(start, s.raw), :]
            out[at + s.raw : at + s.face, :] = halo[pl.ds(mean, s.avg), :]
        if s.ride:
            out[n * s.face :, :] = total.astype(BF16)


def front_kernel(s, field, fine_far, coarse_far, *refs):
    gx = lax.axis_index("gx")
    n, m = len(s.kx), len(s.kz)
    faces, edges, refs = refs[:m], refs[m : m + n], refs[m + n :]
    piece, weights, held, fine, coarse, found, sems = refs
    taps = [
        pltpu.make_async_copy(fine_far, fine, sems.at[s.chunks]),
        pltpu.make_async_copy(coarse_far, coarse, sems.at[s.chunks + 1]),
    ]
    chunk = s.V // s.chunks
    copies = []
    for i in range(s.chunks):
        at = pl.ds(i * chunk, chunk)
        copies.append(pltpu.make_async_copy(field.at[at], held.at[at], sems.at[i]))
    for each in taps + copies:
        each.start()
    half = s.Y // 2
    deep, tall, long = s.Z // s.tz, s.Y // s.ty, s.X // s.tx
    x, lane = iota((s.X, s.V * E), 0), iota((s.X, s.V * E), 1)
    picks = [one(x - jnp.where(upper(gx, kind), s.X - E, 0) == lane % E) for kind in s.kx]
    group = iota((1, s.V * E), 1) // E
    by_v = [
        wide([jnp.where(group == lane_group(s, j, v), p, jnp.zeros_like(p)) for j, p in enumerate(picks)])
        for v in range(s.V)
    ]
    sub = iota((s.V, s.X), 0)
    gz = lax.axis_index("gz")
    row, col = iota((s.avg, s.raw), 0), iota((s.avg, s.raw), 1)
    mean = one((col // s.Y // 2 == row // half) & (col % s.Y // 2 == row % half), 0.25)
    r, c = iota((2 * s.X, s.X), 0), iota((2 * s.X, s.X), 1)
    halve = one(r // 2 == c, 0.5)
    for each in taps:
        each.wait()
    *blocks, pairs_block = x_weights(s, fine, coarse)
    for i, block in enumerate(blocks):
        weights[i] = block
    weights[2, : s.X, : s.X] = pairs_block
    by_vector = [jnp.zeros((s.V, s.X), F32) for _ in range(s.tz * s.ty)]
    stacked = {kind: [] for kind in s.kz}
    for part, copy in enumerate(copies):
        vectors = range(part * chunk, (part + 1) * chunk)
        copy.wait()
        data = wide([held[v].reshape(s.rows, s.X) for v in vectors])
        more = dot(data, jnp.concatenate([by_v[v] for v in vectors], axis=0))
        found[...] = more if part == 0 else found[...] + more
        for kind, out in zip(s.kz, faces):
            up = upper(gz, kind)
            start = jnp.where(up, s.Z - R, 0)
            further = jnp.where(up, s.Z - E, R)
            for v in vectors:
                at = v * s.raw
                out[at : at + s.raw, :] = held[v, pl.ds(start, R)].reshape(s.raw, s.X)
            data = wide([held[v, pl.ds(further, R)].reshape(s.raw, s.X) for v in vectors])
            means = dot(mean, data).astype(BF16)
            for i in range(0, chunk, 2):
                stacked[kind].append(means[:, i * s.X : (i + 2) * s.X])
        for v in vectors:
            for i in range(s.tz):
                layers = held[v, i * deep].astype(F32)
                for z in range(i * deep + 1, (i + 1) * deep):
                    layers = layers + held[v, z].astype(F32)
                for j in range(s.ty):
                    line = jnp.sum(layers[j * tall : (j + 1) * tall], axis=0, keepdims=True)
                    line = jnp.broadcast_to(line * (1.0 / (deep * tall)), (s.V, s.X))
                    by_vector[i * s.ty + j] = jnp.where(sub == v, line, by_vector[i * s.ty + j])
    if faces:
        means = dot(jnp.concatenate([x for kind in s.kz for x in stacked[kind]], axis=0), halve)
        count = s.V // 2 * s.avg
        for i, out in enumerate(faces):
            out[s.V * s.raw :, :] = means[i * count : (i + 1) * count].astype(BF16)
    r, c = iota((2 * s.avg, s.rows), 0), iota((2 * s.avg, s.rows), 1)
    layer = r // half * 2 + jnp.where(r < s.avg, R, s.Z - E - R)
    mean = one((c // s.Y // 2 * 2 == layer) & (c % s.Y // 2 == r % half), 0.25)
    for j in range(n):
        edge = found[:, j * s.V * E : (j + 1) * s.V * E].astype(BF16)
        edges[j][: s.rows, :] = edge
        edges[j][s.rows : s.rows + 2 * s.avg, :] = dot(mean, edge).astype(BF16)
    x, lane = iota((s.X, s.tile), 0), iota((s.X, s.tile), 1)
    for i in range(s.tz):
        total = jnp.zeros((s.V, s.tile), F32)
        for j in range(s.ty):
            spread = jnp.where(lane == (j * s.nx + gx) * s.tx + x // long, 1.0 / long, 0.0)
            total = total + dot(by_vector[i * s.ty + j], spread, precision=lax.Precision.HIGHEST)
        total = total.astype(BF16)
        piece[i * s.V : (i + 1) * s.V, :] = total
        if s.ride:
            for edge in edges:
                at = s.rows + 2 * s.avg + i * s.V
                edge[at : at + s.V, :] = total


def x_weights(s, fine, coarse):
    gx = lax.axis_index("gx")

    def rows(place, count):
        col = iota((count, s.X), 1)
        a = lookup(place - col + R, fine, 2)
        b = 0.5 * lookup((place + E) // 2 - col // 2, coarse, 2)
        return wide([*split(a), b.astype(BF16)])

    half = s.V // 2
    own = rows(iota((s.X, s.X), 0), s.X)
    sides = []
    for kind in s.kx:
        c = iota((E, s.X), 0)
        place = jnp.where(upper(gx, kind), s.X + c, c - E)
        place = jnp.where(partner_missing(gx, s.nx, kind), -4 * s.X, place)
        sides.append(jnp.concatenate([rows(place, E).astype(F32)] * half, axis=0).astype(BF16))
    if len(sides) < 2:
        sides += [jnp.zeros((half * E, 3 * s.X), BF16)] * (2 - len(sides))
    both = [jnp.concatenate([own] + order, axis=0) for order in (sides, sides[::-1])]
    c, col = iota((s.X, s.X), 0) % (s.X // 2), iota((s.X, s.X), 1)
    return both + [lookup(c - col // 2 + R, coarse, 2).astype(BF16)]


def pick_y(s, up, fine):
    if fine:
        r, c = iota((s.yf, s.rows), 0), iota((s.yf, s.rows), 1)
        y0 = jnp.where(up, s.Y - R, 0)
        return one((c // s.Y == r // R) & (c % s.Y == y0 + r % R))
    r, c = iota((s.yc, s.rows), 0), iota((s.yc, s.rows), 1)
    c0 = jnp.where(up, s.Y // 2 - R, 0)
    return one((c // s.Y // 2 == r // R) & (c % s.Y // 2 == c0 + r % R), 0.25)


def pick_zy(s, up, fine):
    half = s.Y // 2
    if fine:
        r, c = iota((s.zyf, s.raw), 0), iota((s.zyf, s.raw), 1)
        y0 = jnp.where(up, s.Y - R, 0)
        return one((c // s.Y == r // R) & (c % s.Y == y0 + r % R))
    r, c = iota((s.zyc, s.face), 0), iota((s.zyc, s.face), 1)
    q, y = r // R, r % R + jnp.where(up, half - R, 0)
    near = (c < s.raw) & (c // s.Y // 2 == q) & (c % s.Y // 2 == y)
    b = c - s.raw
    far = (c >= s.raw) & (b // half + R // 2 == q) & (b % half == y)
    return jnp.where(near, 0.25, jnp.where(far, 1.0, 0.0)).astype(BF16)


def mix(s, halos, v):
    group = iota((1, s.V * E), 1) // E
    mixed = jnp.zeros((halos[0].shape[0] if halos else 0, s.V * E), BF16)
    for i, halo in enumerate(halos):
        mixed = jnp.where(group == lane_group(s, i, v), halo, mixed)
    return mixed


def xpass(s, weights, data, halos, v):
    mixed = mix(s, halos, v) if halos else jnp.zeros((data.shape[0], s.V * E), BF16)
    passed = dot(wide([data, mixed]), weights[v // (s.V // 2)])
    fine = passed[:, : s.X] + passed[:, s.X : 2 * s.X]
    return fine.astype(BF16), passed[:, 2 * s.X :].astype(BF16)


def lane_group(s, place, v):
    return (v + place * (s.V // 2)) % s.V


def own_kernel(s, weights, field, *refs):
    n = len(s.kx)
    halos, (own, *packs) = [h[: s.rows, :] for h in refs[:n]], refs[n:]
    for v in range(s.V):
        at = slice(v * s.X, (v + 1) * s.X)
        fine, coarse = xpass(s, weights, field[v].reshape(s.rows, s.X), halos, v)
        own[: s.rows, at] = fine
        own[s.rows :, at] = coarse
    gy = lax.axis_index("gy")
    for kind, pack in zip(s.ky, packs):
        up = upper(gy, kind)
        pack[: s.yf, :] = dot(pick_y(s, up, True), own[: s.rows, :]).astype(BF16)
        pack[s.yf :, :] = dot(pick_y(s, up, False), own[s.rows :, :]).astype(BF16)


def sides_kernel(s, weights, *refs):
    m = len(s.kz)
    faces, corners, refs = refs[:m], refs[m : 2 * m], refs[2 * m :]
    sides, packs = refs[:m], refs[m:]
    near, far = [], []
    for i in range(len(s.kx)):
        at = i * s.face
        near.append(jnp.concatenate([c[at : at + s.raw, :] for c in corners], axis=0))
        far.append(jnp.concatenate([c[at + s.raw : at + s.face, :] for c in corners], axis=0))
    for v in range(s.V):
        at = slice(v * s.X, (v + 1) * s.X)
        data = jnp.concatenate([f[v * s.raw : (v + 1) * s.raw, :] for f in faces], axis=0)
        fine, coarse = xpass(s, weights, data, near, v)
        for i, side in enumerate(sides):
            rows = slice(i * s.raw, (i + 1) * s.raw)
            side[: s.raw, at] = fine[rows, :]
            side[s.raw : 2 * s.raw, at] = coarse[rows, :]
    right = iota((1, s.X), 1) // (s.X // 2)
    half = s.V // 2
    for h in range(2):
        rows = []
        for v in range(h * half, (h + 1) * half):
            at = s.V * s.raw + v // 2 * s.avg
            data = jnp.concatenate([f[at : at + s.avg, :] for f in faces], axis=0)
            data = jnp.where(right == v % 2, data, jnp.zeros_like(data))
            mixed = mix(s, far, v) if far else jnp.zeros_like(data)
            rows.append(wide([data, mixed]))
        w = jnp.concatenate([weights[2, : s.X, : s.X], weights[h, s.X :, 2 * s.X :]], axis=0)
        passed = dot(jnp.concatenate(rows, axis=0), w).astype(BF16)
        for v in range(h * half, (h + 1) * half):
            for i, side in enumerate(sides):
                at = ((v % half) * len(faces) + i) * s.avg
                side[2 * s.raw :, v * s.X : (v + 1) * s.X] = passed[at : at + s.avg, :]
    gy = lax.axis_index("gy")
    for kind, pack in zip(s.ky, packs):
        up = upper(gy, kind)
        at = 0
        for side in sides:
            pack[at : at + s.zyf, :] = dot(pick_zy(s, up, True), side[: s.raw, :]).astype(BF16)
            at += s.zyf
            pack[at : at + s.zyc, :] = dot(pick_zy(s, up, False), side[s.raw :, :]).astype(BF16)
            at += s.zyc


def yz_weights(s, fine, coarse):
    gy, gz = lax.axis_index("gy"), lax.axis_index("gz")
    half, deep = s.Y // 2, s.Z // 2

    def block(taps, z, y, div, scale=None):
        count = z.shape[1]
        a = lookup(z - iota((s.Z, count), 0) // div + R, taps, 0)
        b = lookup(y - iota((s.Y, count), 0) // div + R, taps, 1)
        if scale is not None:
            b = b * scale
        both = a.reshape(s.Z, 1, count) * b.reshape(1, s.Y, count)
        both = both.reshape(s.rows, count)
        if div == 2:
            return both.astype(BF16)
        high, low = split(both)
        lows.append(low)
        return high

    lows = []

    c = iota((1, s.rows), 1)
    first = [
        block(fine, c // s.Y, c % s.Y, 1),
        block(coarse, c // s.Y // 2, c % s.Y // 2, 2, 0.25),
    ]
    first += [lows.pop()]
    second = []

    def zplace(kind, z):
        return jnp.where(partner_missing(gz, s.nz, kind), -4 * s.Z, z)

    for kind in s.ky:
        up = upper(gy, kind)
        c = iota((1, s.yf), 1)
        second.append(block(fine, c // R, c % R + jnp.where(up, s.Y, -R), 1))
        c = iota((1, s.yc), 1)
        second.append(block(coarse, c // R, c % R + jnp.where(up, half, -R), 2))
    for kind in s.kz:
        up = upper(gz, kind)
        c = iota((1, s.raw), 1)
        second.append(block(fine, zplace(kind, c // s.Y + jnp.where(up, s.Z, -R)), c % s.Y, 1))
        c = iota((1, s.face), 1)
        b = c - s.raw
        near = c // s.Y // 2 + jnp.where(up, deep, -R // 2)
        far = b // half + jnp.where(up, deep + R // 2, -R)
        z = zplace(kind, jnp.where(c < s.raw, near, far))
        y = jnp.where(c < s.raw, c % s.Y // 2, b % half)
        second.append(block(coarse, z, y, 2, jnp.where(c < s.raw, 0.25, 1.0)))
    for kind in s.ky:
        up = upper(gy, kind)
        fy, cy = jnp.where(up, s.Y, -R), jnp.where(up, half, -R)
        for zkind in s.kz:
            zup = upper(gz, zkind)
            c = iota((1, s.zyf), 1)
            z = zplace(zkind, c // R + jnp.where(zup, s.Z, -R))
            second.append(block(fine, z, c % R + fy, 1))
            c = iota((1, s.zyc), 1)
            q = c // R
            near = q + jnp.where(zup, deep, -R // 2)
            far = q - R // 2 + jnp.where(zup, deep + R // 2, -R)
            z = zplace(zkind, jnp.where(q < R // 2, near, far))
            second.append(block(coarse, z, c % R + cy, 2))
    r, c = iota((s.rows, s.top), 0), iota((s.rows, s.top), 1)
    z, y = r // s.Y // (s.Z // s.tz), r % s.Y // (s.Y // s.ty)
    second.append(one(c // s.tx == z * s.ty + y))
    return first, second + lows


def top_product(s, kernel, parts, total):
    for z, y, part in parts:
        for i in range(s.tz):
            q = pl.multiple_of(((z * s.tz + i) * s.ny + y) * s.tile, s.tile)
            rows = part(slice(i * s.V, (i + 1) * s.V), i)
            total = total + dot(kernel[:, pl.ds(q, s.tile)], rows, ((1,), (1,)))
    return total


def weights_kernel(s, fine, coarse, now, later):
    first, second = yz_weights(s, fine, coarse)
    for ref, blocks in ((now, first), (later, second)):
        at = 0
        for block in blocks:
            ref[:, at : at + block.shape[1]] = block
            at += block.shape[1]


def partial_kernel(s, now, own, total):
    step = min(s.lanes, 4 * s.X)
    for at in range(0, s.lanes, step):
        cols = slice(at, at + step)
        parts = [own[:, cols], own[: s.rows, cols]]
        total[:, cols] = dot(now[...], jnp.concatenate(parts, axis=0))


def top_own_kernel(s, known, kernel, total):
    gy, gz = lax.axis_index("gy"), lax.axis_index("gz")
    parts = [(slot(z, gz, s.nz), gy, lambda at, i, z=z: known[z, at, :]) for z in range(s.nz)]
    total[...] = top_product(s, kernel, parts, jnp.zeros((s.top, s.V), F32))


def final_kernel(s, *refs):
    m, k = len(s.kz), len(s.ky)
    partial, later, *refs = refs
    ends, refs = refs[:k], refs[k:]
    sides, refs = refs[:m], refs[m:]
    packs, refs = refs[:k], refs[k:]
    started, known, kernel, out, held, sems = refs
    gy, gz = lax.axis_index("gy"), lax.axis_index("gz")
    parts = [
        (slot(z, gz, s.nz), slot(y, gy, s.ny), lambda at, i, y=y, z=z: known[y, z, at, :])
        for y in range(1 if doubling(s.ny) else 0, s.ny)
        for z in range(s.nz)
    ]
    total = top_product(s, kernel, parts, started[...])
    r, c = iota((s.top, s.X), 0), iota((s.top, s.X), 1)
    spread = c // (s.X // s.tx) == r % s.tx
    chunk = s.V // s.chunks
    copies = []
    pair = 2 if chunk % 2 == 0 else 1
    for v in range(0, s.V, pair):
        cols = slice(v * s.X, (v + pair) * s.X)
        lines = [jnp.broadcast_to(total[:, v + i : v + i + 1], (s.top, s.X)) for i in range(pair)]
        top = wide([jnp.where(spread, line, 0.0).astype(BF16) for line in lines])
        parts = [x[:, cols] for x in (*ends, *sides)]
        parts += [x[:, cols] for x in packs] + [top]
        parts += [x[: s.yf, cols] for x in ends] + [x[: s.raw, cols] for x in sides]
        step = s.zyf + s.zyc
        parts += [x[j * step : j * step + s.zyf, cols] for x in packs for j in range(m)]
        result = (dot(later[...], jnp.concatenate(parts, axis=0)) + partial[:, cols]).astype(BF16)
        for i in range(pair):
            held[v + i] = result[:, i * s.X : (i + 1) * s.X].reshape(s.Z, s.Y, s.X)
        if (v + pair) % chunk == 0:
            at = pl.ds(v + pair - chunk, chunk)
            copies.append(pltpu.make_async_copy(held.at[at], out.at[at], sems.at[v // chunk]))
            copies[-1].start()
    for copy in copies:
        copy.wait()


def doubling(count):
    return count & (count - 1) == 0


def slot(place, me, count):
    return place ^ me if doubling(count) else place


def gather(a, axis, count, join):
    if not doubling(count):
        return join(list(lax.all_gather(a, axis)))
    step = 1
    while step < count:
        a = join([a, lax.ppermute(a, axis, [(i, i ^ step) for i in range(count)])])
        step *= 2
    return a


def shape(*dims):
    return jax.ShapeDtypeStruct(dims, BF16)


def bind(body, s):
    def kernel(*refs):
        body(s, *refs)

    kernel.__name__ = body.__name__
    return kernel


def shards(sizes, field, fine_taps, coarse_taps, top_kernel):
    s = Sizes(field.shape, top_kernel.shape[:3], sizes)
    n, m, k = len(s.kx), len(s.kz), len(s.ky)

    def run(body, arrays, outs, scalars=0, scratch=(), flops=0, far=(), far_out=False):
        specs = [vmem()] * len(arrays)
        for i in range(scalars):
            specs[i] = smem()
        for i in far:
            specs[i] = pl.BlockSpec(memory_space=pltpu.HBM)
        call = pl.pallas_call(
            bind(body, s),
            out_shape=outs,
            in_specs=specs,
            out_specs=[pl.BlockSpec(memory_space=pltpu.HBM) if far_out else vmem()] * len(outs),
            scratch_shapes=scratch,
            compiler_params=pltpu.CompilerParams(vmem_limit_bytes=24 << 20),
            cost_estimate=pl.CostEstimate(flops=flops, bytes_accessed=1 << 20, transcendentals=0),
        )
        return list(call(*arrays))

    def swap(arrays, axis, count, which, ring=False):
        moved = []
        for a, kind in zip(arrays, which):
            moved.append(lax.ppermute(a, axis, swaps(count, kind, ring)))
        return moved

    taps = [fine_taps, coarse_taps]
    buffers = [pltpu.VMEM(field.shape, BF16), pltpu.SemaphoreType.DMA((s.chunks,))]
    top = shape(s.tz * s.V, s.tile)
    x_depth = s.X + s.V * E
    outs = [shape(s.sent, s.X)] * m + [shape(s.edge, s.V * E)] * n
    outs += [top, shape(3, x_depth, 3 * s.X), shape(*field.shape)]
    far = [pltpu.with_memory_space_constraint(a, pltpu.HBM) for a in (field, *taps)]
    *faces, piece, weights, field = run(
        front_kernel,
        far,
        outs,
        scratch=[pltpu.SMEM(a.shape, a.dtype) for a in taps]
        + [
            pltpu.VMEM((s.rows, max(n, 1) * s.V * E), F32),
            pltpu.SemaphoreType.DMA((s.chunks + 2,)),
        ],
        far=(0, 1, 2),
    )
    faces, edges = faces[:m], faces[m:]
    halos = swap(edges, "gx", s.nx, s.kx, s.ride)
    faces = swap(faces, "gz", s.nz, s.kz)
    corner = [shape(s.corner, s.V * E)] * m
    stack = lambda parts: jnp.concatenate(parts, axis=0)
    if s.ride:
        across = lax.ppermute(piece, "gx", [(i, i ^ 2) for i in range(s.nx)])
        *corners, known = run(corners_kernel, halos + [piece, across], corner + [top])
    else:
        corners = run(corners_kernel, halos, corner)
    corners = swap(corners, "gz", s.nz, s.kz, s.ride)
    if s.ride:
        across = lax.ppermute(known, "gz", [(i, i ^ 2) for i in range(s.nz)])
        near, far = [c[n * s.face :] for c in corners]
        known = jnp.stack([known, near, across, far])
    else:
        known = gather(gather(piece, "gx", s.nx, sum)[None], "gz", s.nz, stack)
    later = k * (s.yf + s.yc) + m * s.gz + k * s.ypack + s.top
    later += k * s.yf + m * s.raw + k * m * s.zyf
    w_now, w_later = run(
        weights_kernel,
        taps,
        [shape(s.rows, 3 * s.rows), shape(s.rows, later)],
        scalars=2,
        flops=1 << 28,
    )
    own, *ends = run(
        own_kernel,
        [weights, field] + halos,
        [shape(2 * s.rows, s.lanes)] + [shape(s.yf + s.yc, s.lanes)] * k,
        flops=4 * s.rows * s.V * x_depth * s.X,
    )
    ends = swap(ends, "gy", s.ny, s.ky)
    rest = run(
        sides_kernel,
        [weights] + faces + corners,
        [shape(s.gz, s.lanes)] * m + [shape(s.ypack, s.lanes)] * k,
    )
    sides, packs = rest[:m], rest[m:]
    packs = swap(packs, "gy", s.ny, s.ky)
    partial = run(
        partial_kernel,
        [w_now, own],
        [jax.ShapeDtypeStruct((s.rows, s.lanes), F32)],
        flops=4 * s.rows * s.rows * s.lanes,
    )[0]
    kernel_rows = top_kernel.reshape(s.top, top_kernel.shape[3])
    started = jnp.zeros((s.top, s.V), F32)
    if doubling(s.ny):
        started = run(
            top_own_kernel, [known, kernel_rows], [jax.ShapeDtypeStruct((s.top, s.V), F32)]
        )[0]
    known = gather(known[None], "gy", s.ny, stack)
    return run(
        final_kernel,
        [partial, w_later] + ends + sides + packs + [started, known, kernel_rows],
        [shape(*field.shape)],
        scratch=buffers,
        far_out=True,
    )[0]


def solution(mesh):
    sizes = tuple(mesh.shape[name] for name in ("gx", "gy", "gz"))

    def body(*args):
        return shards(sizes, *args)

    return jax.shard_map(
        body,
        mesh=mesh,
        in_specs=(P(None, "gz", "gy", "gx"), P(), P(), P("gz", "gy", "gx", None)),
        out_specs=P(None, "gz", "gy", "gx"),
        check_vma=False,
    )
```

```python
import jax
import jax.numpy as jnp
from jax import lax
from jax.experimental import pallas as pl
from jax.experimental.pallas import tpu as pltpu
from jax.sharding import PartitionSpec as P


F32 = jnp.float32
BF16 = jnp.bfloat16
R = 4
E = 2 * R


def swaps(count, kind, ring=False):
    pairs = []
    for i in range(kind, count - 1, 2):
        pairs += [(i, i + 1), (i + 1, i)]
    if ring and kind == 1 and pairs and count % 2 == 0:
        pairs += [(0, count - 1), (count - 1, 0)]
    return pairs


def partner_missing(index, count, kind):
    at = index + jnp.where(upper(index, kind), 1, -1)
    return (at < 0) | (at >= count)


def kinds(count):
    return [k for k in (0, 1) if swaps(count, k)]


def upper(index, kind):
    return lax.rem(index + kind, 2) == 0


def iota(shape, dim):
    return lax.broadcasted_iota(jnp.int32, shape, dim)


def dot(a, b, dims=((1,), (0,)), precision=None):
    return lax.dot_general(a, b, (dims, ((), ())), precision=precision, preferred_element_type=F32)


def lookup(offset, taps, row):
    total = jnp.zeros(offset.shape, F32)
    for k in range(2 * R + 1):
        total = jnp.where(offset == k, taps[row, k], total)
    return total


def one(condition, value=1.0):
    return jnp.where(condition, value, 0.0).astype(BF16)


def split(a):
    high = a.astype(BF16)
    return high, (a - high.astype(F32)).astype(BF16)


def wide(parts):
    return jnp.concatenate(parts, axis=1)


class Sizes:
    def __init__(self, shape, top_shape, mesh_sizes):
        self.V, self.Z, self.Y, self.X = shape
        self.nx, self.ny, self.nz = mesh_sizes
        self.rows = self.Z * self.Y
        self.lanes = self.V * self.X
        self.raw = R * self.Y
        self.avg = (R // 2) * (self.Y // 2)
        self.face = self.raw + self.avg
        self.kx, self.ky, self.kz = kinds(self.nx), kinds(self.ny), kinds(self.nz)
        self.yf, self.yc = self.Z * R, (self.Z // 2) * R
        self.zyf, self.zyc = R * R, R * R
        self.tz, self.ty, self.tx = top_shape
        self.top = self.tz * self.ty * self.tx
        self.gz = self.raw + self.face
        self.sent = self.V * self.raw + self.V // 2 * self.avg
        self.tile = self.ty * self.tx * self.nx
        self.ride = self.nx == 4 and self.nz == 4 and self.tile == self.V * E
        self.edge = self.rows + 2 * self.avg + (self.tz * self.V if self.ride else 0)
        self.ypack = len(self.kz) * (self.zyf + self.zyc)
        self.front = 2 if self.V % 4 == 0 else 1
        self.chunks = 4 if self.V % 4 == 0 else 1
        self.corner = len(self.kx) * self.face + (self.tz * self.V if self.ride else 0)


def smem():
    return pl.BlockSpec(memory_space=pltpu.SMEM)


def vmem():
    return pl.BlockSpec(memory_space=pltpu.VMEM)


def corners_kernel(s, *refs):
    me = lax.axis_index("gz")
    n = len(s.kx)
    halos, refs = refs[:n], refs[n:]
    if s.ride:
        piece, across, *outs, known = refs
        total = piece[...].astype(F32) + across[...].astype(F32)
        for halo in halos:
            total = total + halo[s.rows + 2 * s.avg :, :].astype(F32)
        known[...] = total.astype(BF16)
    else:
        outs = refs
    for kind, out in zip(s.kz, outs):
        up = upper(me, kind)
        start = pl.multiple_of(jnp.where(up, s.rows - s.raw, 0), 16)
        mean = pl.multiple_of(jnp.where(up, s.rows + s.avg, s.rows), 16)
        for i, halo in enumerate(halos):
            at = i * s.face
            out[at : at + s.raw, :] = halo[pl.ds(start, s.raw), :]
            out[at + s.raw : at + s.face, :] = halo[pl.ds(mean, s.avg), :]
        if s.ride:
            out[n * s.face :, :] = total.astype(BF16)


def front_kernel(s, field, fine_far, coarse_far, *refs):
    gx = lax.axis_index("gx")
    n, m = len(s.kx), len(s.kz)
    faces, edges, refs = refs[:m], refs[m : m + n], refs[m + n :]
    piece, weights, held, fine, coarse, found, sems = refs
    taps = [
        pltpu.make_async_copy(fine_far, fine, sems.at[s.front]),
        pltpu.make_async_copy(coarse_far, coarse, sems.at[s.front + 1]),
    ]
    chunk = s.V // s.front
    copies = []
    for i in range(s.front):
        at = pl.ds(i * chunk, chunk)
        copies.append(pltpu.make_async_copy(field.at[at], held.at[at], sems.at[i]))
    for each in taps + copies:
        each.start()
    half = s.Y // 2
    deep, tall, long = s.Z // s.tz, s.Y // s.ty, s.X // s.tx
    x, lane = iota((s.X, s.V * E), 0), iota((s.X, s.V * E), 1)
    picks = [one(x - jnp.where(upper(gx, kind), s.X - E, 0) == lane % E) for kind in s.kx]
    group = iota((1, s.V * E), 1) // E
    by_v = [
        wide([jnp.where(group == lane_group(s, j, v), p, jnp.zeros_like(p)) for j, p in enumerate(picks)])
        for v in range(s.V)
    ]
    sub = iota((s.V, s.X), 0)
    gz = lax.axis_index("gz")
    row, col = iota((s.avg, s.raw), 0), iota((s.avg, s.raw), 1)
    mean = one((col // s.Y // 2 == row // half) & (col % s.Y // 2 == row % half), 0.25)
    r, c = iota((2 * s.X, s.X), 0), iota((2 * s.X, s.X), 1)
    halve = one(r // 2 == c, 0.5)
    for each in taps:
        each.wait()
    *blocks, pairs_block = x_weights(s, fine, coarse)
    for i, block in enumerate(blocks):
        weights[i] = block
    weights[2, : s.X, : s.X] = pairs_block
    by_vector = [jnp.zeros((s.V, s.X), F32) for _ in range(s.tz * s.ty)]
    stacked = {kind: [] for kind in s.kz}
    for part, copy in enumerate(copies):
        vectors = range(part * chunk, (part + 1) * chunk)
        copy.wait()
        data = wide([held[v].reshape(s.rows, s.X) for v in vectors])
        more = dot(data, jnp.concatenate([by_v[v] for v in vectors], axis=0))
        found[...] = more if part == 0 else found[...] + more
        for kind, out in zip(s.kz, faces):
            up = upper(gz, kind)
            start = jnp.where(up, s.Z - R, 0)
            further = jnp.where(up, s.Z - E, R)
            for v in vectors:
                at = v * s.raw
                out[at : at + s.raw, :] = held[v, pl.ds(start, R)].reshape(s.raw, s.X)
            data = wide([held[v, pl.ds(further, R)].reshape(s.raw, s.X) for v in vectors])
            means = dot(mean, data).astype(BF16)
            for i in range(0, chunk, 2):
                stacked[kind].append(means[:, i * s.X : (i + 2) * s.X])
        for v in vectors:
            for i in range(s.tz):
                layers = held[v, i * deep].astype(F32)
                for z in range(i * deep + 1, (i + 1) * deep):
                    layers = layers + held[v, z].astype(F32)
                for j in range(s.ty):
                    line = jnp.sum(layers[j * tall : (j + 1) * tall], axis=0, keepdims=True)
                    line = jnp.broadcast_to(line * (1.0 / (deep * tall)), (s.V, s.X))
                    by_vector[i * s.ty + j] = jnp.where(sub == v, line, by_vector[i * s.ty + j])
    if faces:
        means = dot(jnp.concatenate([x for kind in s.kz for x in stacked[kind]], axis=0), halve)
        count = s.V // 2 * s.avg
        for i, out in enumerate(faces):
            out[s.V * s.raw :, :] = means[i * count : (i + 1) * count].astype(BF16)
    r, c = iota((2 * s.avg, s.rows), 0), iota((2 * s.avg, s.rows), 1)
    layer = r // half * 2 + jnp.where(r < s.avg, R, s.Z - E - R)
    mean = one((c // s.Y // 2 * 2 == layer) & (c % s.Y // 2 == r % half), 0.25)
    for j in range(n):
        edge = found[:, j * s.V * E : (j + 1) * s.V * E].astype(BF16)
        edges[j][: s.rows, :] = edge
        edges[j][s.rows : s.rows + 2 * s.avg, :] = dot(mean, edge).astype(BF16)
    x, lane = iota((s.X, s.tile), 0), iota((s.X, s.tile), 1)
    for i in range(s.tz):
        total = jnp.zeros((s.V, s.tile), F32)
        for j in range(s.ty):
            spread = jnp.where(lane == (j * s.nx + gx) * s.tx + x // long, 1.0 / long, 0.0)
            total = total + dot(by_vector[i * s.ty + j], spread, precision=lax.Precision.HIGHEST)
        total = total.astype(BF16)
        piece[i * s.V : (i + 1) * s.V, :] = total
        if s.ride:
            for edge in edges:
                at = s.rows + 2 * s.avg + i * s.V
                edge[at : at + s.V, :] = total


def x_weights(s, fine, coarse):
    gx = lax.axis_index("gx")

    def rows(place, count):
        col = iota((count, s.X), 1)
        a = lookup(place - col + R, fine, 2)
        b = 0.5 * lookup((place + E) // 2 - col // 2, coarse, 2)
        return wide([*split(a), b.astype(BF16)])

    half = s.V // 2
    own = rows(iota((s.X, s.X), 0), s.X)
    sides = []
    for kind in s.kx:
        c = iota((E, s.X), 0)
        place = jnp.where(upper(gx, kind), s.X + c, c - E)
        place = jnp.where(partner_missing(gx, s.nx, kind), -4 * s.X, place)
        sides.append(jnp.concatenate([rows(place, E).astype(F32)] * half, axis=0).astype(BF16))
    if len(sides) < 2:
        sides += [jnp.zeros((half * E, 3 * s.X), BF16)] * (2 - len(sides))
    both = [jnp.concatenate([own] + order, axis=0) for order in (sides, sides[::-1])]
    c, col = iota((s.X, s.X), 0) % (s.X // 2), iota((s.X, s.X), 1)
    return both + [lookup(c - col // 2 + R, coarse, 2).astype(BF16)]


def pick_y(s, up, fine):
    if fine:
        r, c = iota((s.yf, s.rows), 0), iota((s.yf, s.rows), 1)
        y0 = jnp.where(up, s.Y - R, 0)
        return one((c // s.Y == r // R) & (c % s.Y == y0 + r % R))
    r, c = iota((s.yc, s.rows), 0), iota((s.yc, s.rows), 1)
    c0 = jnp.where(up, s.Y // 2 - R, 0)
    return one((c // s.Y // 2 == r // R) & (c % s.Y // 2 == c0 + r % R), 0.25)


def pick_zy(s, up, fine):
    half = s.Y // 2
    if fine:
        r, c = iota((s.zyf, s.raw), 0), iota((s.zyf, s.raw), 1)
        y0 = jnp.where(up, s.Y - R, 0)
        return one((c // s.Y == r // R) & (c % s.Y == y0 + r % R))
    r, c = iota((s.zyc, s.face), 0), iota((s.zyc, s.face), 1)
    q, y = r // R, r % R + jnp.where(up, half - R, 0)
    near = (c < s.raw) & (c // s.Y // 2 == q) & (c % s.Y // 2 == y)
    b = c - s.raw
    far = (c >= s.raw) & (b // half + R // 2 == q) & (b % half == y)
    return jnp.where(near, 0.25, jnp.where(far, 1.0, 0.0)).astype(BF16)


def mix(s, halos, v):
    group = iota((1, s.V * E), 1) // E
    mixed = jnp.zeros((halos[0].shape[0] if halos else 0, s.V * E), BF16)
    for i, halo in enumerate(halos):
        mixed = jnp.where(group == lane_group(s, i, v), halo, mixed)
    return mixed


def xpass(s, weights, data, halos, v):
    mixed = mix(s, halos, v) if halos else jnp.zeros((data.shape[0], s.V * E), BF16)
    passed = dot(wide([data, mixed]), weights[v // (s.V // 2)])
    fine = passed[:, : s.X] + passed[:, s.X : 2 * s.X]
    return fine.astype(BF16), passed[:, 2 * s.X :].astype(BF16)


def lane_group(s, place, v):
    return (v + place * (s.V // 2)) % s.V


def own_kernel(s, weights, field, *refs):
    n = len(s.kx)
    halos, (own, *packs) = [h[: s.rows, :] for h in refs[:n]], refs[n:]
    for v in range(s.V):
        at = slice(v * s.X, (v + 1) * s.X)
        fine, coarse = xpass(s, weights, field[v].reshape(s.rows, s.X), halos, v)
        own[: s.rows, at] = fine
        own[s.rows :, at] = coarse
    gy = lax.axis_index("gy")
    for kind, pack in zip(s.ky, packs):
        up = upper(gy, kind)
        pack[: s.yf, :] = dot(pick_y(s, up, True), own[: s.rows, :]).astype(BF16)
        pack[s.yf :, :] = dot(pick_y(s, up, False), own[s.rows :, :]).astype(BF16)


def sides_kernel(s, weights, *refs):
    m = len(s.kz)
    faces, corners, refs = refs[:m], refs[m : 2 * m], refs[2 * m :]
    sides, packs = refs[:m], refs[m:]
    near, far = [], []
    for i in range(len(s.kx)):
        at = i * s.face
        near.append(jnp.concatenate([c[at : at + s.raw, :] for c in corners], axis=0))
        far.append(jnp.concatenate([c[at + s.raw : at + s.face, :] for c in corners], axis=0))
    for v in range(s.V):
        at = slice(v * s.X, (v + 1) * s.X)
        data = jnp.concatenate([f[v * s.raw : (v + 1) * s.raw, :] for f in faces], axis=0)
        fine, coarse = xpass(s, weights, data, near, v)
        for i, side in enumerate(sides):
            rows = slice(i * s.raw, (i + 1) * s.raw)
            side[: s.raw, at] = fine[rows, :]
            side[s.raw : 2 * s.raw, at] = coarse[rows, :]
    right = iota((1, s.X), 1) // (s.X // 2)
    half = s.V // 2
    for h in range(2):
        rows = []
        for v in range(h * half, (h + 1) * half):
            at = s.V * s.raw + v // 2 * s.avg
            data = jnp.concatenate([f[at : at + s.avg, :] for f in faces], axis=0)
            data = jnp.where(right == v % 2, data, jnp.zeros_like(data))
            mixed = mix(s, far, v) if far else jnp.zeros_like(data)
            rows.append(wide([data, mixed]))
        w = jnp.concatenate([weights[2, : s.X, : s.X], weights[h, s.X :, 2 * s.X :]], axis=0)
        passed = dot(jnp.concatenate(rows, axis=0), w).astype(BF16)
        for v in range(h * half, (h + 1) * half):
            for i, side in enumerate(sides):
                at = ((v % half) * len(faces) + i) * s.avg
                side[2 * s.raw :, v * s.X : (v + 1) * s.X] = passed[at : at + s.avg, :]
    gy = lax.axis_index("gy")
    for kind, pack in zip(s.ky, packs):
        up = upper(gy, kind)
        at = 0
        for side in sides:
            pack[at : at + s.zyf, :] = dot(pick_zy(s, up, True), side[: s.raw, :]).astype(BF16)
            at += s.zyf
            pack[at : at + s.zyc, :] = dot(pick_zy(s, up, False), side[s.raw :, :]).astype(BF16)
            at += s.zyc


def yz_weights(s, fine, coarse):
    gy, gz = lax.axis_index("gy"), lax.axis_index("gz")
    half, deep = s.Y // 2, s.Z // 2

    def block(taps, z, y, div, scale=None):
        count = z.shape[1]
        a = lookup(z - iota((s.Z, count), 0) // div + R, taps, 0)
        b = lookup(y - iota((s.Y, count), 0) // div + R, taps, 1)
        if scale is not None:
            b = b * scale
        both = a.reshape(s.Z, 1, count) * b.reshape(1, s.Y, count)
        both = both.reshape(s.rows, count)
        if div == 2:
            return both.astype(BF16)
        high, low = split(both)
        lows.append(low)
        return high

    lows = []

    c = iota((1, s.rows), 1)
    first = [
        block(fine, c // s.Y, c % s.Y, 1),
        block(coarse, c // s.Y // 2, c % s.Y // 2, 2, 0.25),
    ]
    first += [lows.pop()]
    second = []

    def zplace(kind, z):
        return jnp.where(partner_missing(gz, s.nz, kind), -4 * s.Z, z)

    for kind in s.ky:
        up = upper(gy, kind)
        c = iota((1, s.yf), 1)
        second.append(block(fine, c // R, c % R + jnp.where(up, s.Y, -R), 1))
        c = iota((1, s.yc), 1)
        second.append(block(coarse, c // R, c % R + jnp.where(up, half, -R), 2))
    for kind in s.kz:
        up = upper(gz, kind)
        c = iota((1, s.raw), 1)
        second.append(block(fine, zplace(kind, c // s.Y + jnp.where(up, s.Z, -R)), c % s.Y, 1))
        c = iota((1, s.face), 1)
        b = c - s.raw
        near = c // s.Y // 2 + jnp.where(up, deep, -R // 2)
        far = b // half + jnp.where(up, deep + R // 2, -R)
        z = zplace(kind, jnp.where(c < s.raw, near, far))
        y = jnp.where(c < s.raw, c % s.Y // 2, b % half)
        second.append(block(coarse, z, y, 2, jnp.where(c < s.raw, 0.25, 1.0)))
    for kind in s.ky:
        up = upper(gy, kind)
        fy, cy = jnp.where(up, s.Y, -R), jnp.where(up, half, -R)
        for zkind in s.kz:
            zup = upper(gz, zkind)
            c = iota((1, s.zyf), 1)
            z = zplace(zkind, c // R + jnp.where(zup, s.Z, -R))
            second.append(block(fine, z, c % R + fy, 1))
            c = iota((1, s.zyc), 1)
            q = c // R
            near = q + jnp.where(zup, deep, -R // 2)
            far = q - R // 2 + jnp.where(zup, deep + R // 2, -R)
            z = zplace(zkind, jnp.where(q < R // 2, near, far))
            second.append(block(coarse, z, c % R + cy, 2))
    r, c = iota((s.rows, s.top), 0), iota((s.rows, s.top), 1)
    z, y = r // s.Y // (s.Z // s.tz), r % s.Y // (s.Y // s.ty)
    second.append(one(c // s.tx == z * s.ty + y))
    return first, second + lows


def top_product(s, kernel, parts, total):
    for z, y, part in parts:
        for i in range(s.tz):
            q = pl.multiple_of(((z * s.tz + i) * s.ny + y) * s.tile, s.tile)
            rows = part(slice(i * s.V, (i + 1) * s.V), i)
            total = total + dot(kernel[:, pl.ds(q, s.tile)], rows, ((1,), (1,)))
    return total


def weights_kernel(s, fine, coarse, now, later):
    first, second = yz_weights(s, fine, coarse)
    for ref, blocks in ((now, first), (later, second)):
        at = 0
        for block in blocks:
            ref[:, at : at + block.shape[1]] = block
            at += block.shape[1]


def partial_kernel(s, now, own, total):
    step = min(s.lanes, 4 * s.X)
    for at in range(0, s.lanes, step):
        cols = slice(at, at + step)
        parts = [own[:, cols], own[: s.rows, cols]]
        total[:, cols] = dot(now[...], jnp.concatenate(parts, axis=0))


def top_own_kernel(s, known, kernel, total):
    gy, gz = lax.axis_index("gy"), lax.axis_index("gz")
    parts = [(slot(z, gz, s.nz), gy, lambda at, i, z=z: known[z, at, :]) for z in range(s.nz)]
    total[...] = top_product(s, kernel, parts, jnp.zeros((s.top, s.V), F32))


def final_kernel(s, *refs):
    m, k = len(s.kz), len(s.ky)
    partial, later, *refs = refs
    ends, refs = refs[:k], refs[k:]
    sides, refs = refs[:m], refs[m:]
    packs, refs = refs[:k], refs[k:]
    started, known, kernel, out, held, sems = refs
    gy, gz = lax.axis_index("gy"), lax.axis_index("gz")
    parts = [
        (slot(z, gz, s.nz), slot(y, gy, s.ny), lambda at, i, y=y, z=z: known[y, z, at, :])
        for y in range(1 if doubling(s.ny) else 0, s.ny)
        for z in range(s.nz)
    ]
    total = top_product(s, kernel, parts, started[...])
    r, c = iota((s.top, s.X), 0), iota((s.top, s.X), 1)
    spread = c // (s.X // s.tx) == r % s.tx
    chunk = s.V // s.chunks
    copies = []
    pair = 2 if chunk % 2 == 0 else 1
    for v in range(0, s.V, pair):
        cols = slice(v * s.X, (v + pair) * s.X)
        lines = [jnp.broadcast_to(total[:, v + i : v + i + 1], (s.top, s.X)) for i in range(pair)]
        top = wide([jnp.where(spread, line, 0.0).astype(BF16) for line in lines])
        parts = [x[:, cols] for x in (*ends, *sides)]
        parts += [x[:, cols] for x in packs] + [top]
        parts += [x[: s.yf, cols] for x in ends] + [x[: s.raw, cols] for x in sides]
        step = s.zyf + s.zyc
        parts += [x[j * step : j * step + s.zyf, cols] for x in packs for j in range(m)]
        result = (dot(later[...], jnp.concatenate(parts, axis=0)) + partial[:, cols]).astype(BF16)
        for i in range(pair):
            held[v + i] = result[:, i * s.X : (i + 1) * s.X].reshape(s.Z, s.Y, s.X)
        if (v + pair) % chunk == 0:
            at = pl.ds(v + pair - chunk, chunk)
            copies.append(pltpu.make_async_copy(held.at[at], out.at[at], sems.at[v // chunk]))
            copies[-1].start()
    for copy in copies:
        copy.wait()


def doubling(count):
    return count & (count - 1) == 0


def slot(place, me, count):
    return place ^ me if doubling(count) else place


def gather(a, axis, count, join):
    if not doubling(count):
        return join(list(lax.all_gather(a, axis)))
    step = 1
    while step < count:
        a = join([a, lax.ppermute(a, axis, [(i, i ^ step) for i in range(count)])])
        step *= 2
    return a


def shape(*dims):
    return jax.ShapeDtypeStruct(dims, BF16)


def bind(body, s):
    def kernel(*refs):
        body(s, *refs)

    kernel.__name__ = body.__name__
    return kernel


def shards(sizes, field, fine_taps, coarse_taps, top_kernel):
    s = Sizes(field.shape, top_kernel.shape[:3], sizes)
    n, m, k = len(s.kx), len(s.kz), len(s.ky)

    def run(body, arrays, outs, scalars=0, scratch=(), flops=0, far=(), far_out=False):
        specs = [vmem()] * len(arrays)
        for i in range(scalars):
            specs[i] = smem()
        for i in far:
            specs[i] = pl.BlockSpec(memory_space=pltpu.HBM)
        call = pl.pallas_call(
            bind(body, s),
            out_shape=outs,
            in_specs=specs,
            out_specs=[pl.BlockSpec(memory_space=pltpu.HBM) if far_out else vmem()] * len(outs),
            scratch_shapes=scratch,
            compiler_params=pltpu.CompilerParams(vmem_limit_bytes=24 << 20),
            cost_estimate=pl.CostEstimate(flops=flops, bytes_accessed=1 << 20, transcendentals=0),
        )
        return list(call(*arrays))

    def swap(arrays, axis, count, which, ring=False):
        moved = []
        for a, kind in zip(arrays, which):
            moved.append(lax.ppermute(a, axis, swaps(count, kind, ring)))
        return moved

    taps = [fine_taps, coarse_taps]
    buffers = [pltpu.VMEM(field.shape, BF16), pltpu.SemaphoreType.DMA((s.chunks,))]
    top = shape(s.tz * s.V, s.tile)
    x_depth = s.X + s.V * E
    outs = [shape(s.sent, s.X)] * m + [shape(s.edge, s.V * E)] * n
    outs += [top, shape(3, x_depth, 3 * s.X), shape(*field.shape)]
    far = [pltpu.with_memory_space_constraint(a, pltpu.HBM) for a in (field, *taps)]
    *faces, piece, weights, field = run(
        front_kernel,
        far,
        outs,
        scratch=[pltpu.SMEM(a.shape, a.dtype) for a in taps]
        + [pltpu.VMEM((s.rows, max(n, 1) * s.V * E), F32), pltpu.SemaphoreType.DMA((s.front + 2,))],
        far=(0, 1, 2),
    )
    faces, edges = faces[:m], faces[m:]
    halos = swap(edges, "gx", s.nx, s.kx, s.ride)
    faces = swap(faces, "gz", s.nz, s.kz)
    corner = [shape(s.corner, s.V * E)] * m
    stack = lambda parts: jnp.concatenate(parts, axis=0)
    if s.ride:
        across = lax.ppermute(piece, "gx", [(i, i ^ 2) for i in range(s.nx)])
        *corners, known = run(corners_kernel, halos + [piece, across], corner + [top])
    else:
        corners = run(corners_kernel, halos, corner)
    corners = swap(corners, "gz", s.nz, s.kz, s.ride)
    if s.ride:
        across = lax.ppermute(known, "gz", [(i, i ^ 2) for i in range(s.nz)])
        near, far = [c[n * s.face :] for c in corners]
        known = jnp.stack([known, near, across, far])
    else:
        known = gather(gather(piece, "gx", s.nx, sum)[None], "gz", s.nz, stack)
    later = k * (s.yf + s.yc) + m * s.gz + k * s.ypack + s.top
    later += k * s.yf + m * s.raw + k * m * s.zyf
    w_now, w_later = run(
        weights_kernel,
        taps,
        [shape(s.rows, 3 * s.rows), shape(s.rows, later)],
        scalars=2,
        flops=1 << 28,
    )
    own, *ends = run(
        own_kernel,
        [weights, field] + halos,
        [shape(2 * s.rows, s.lanes)] + [shape(s.yf + s.yc, s.lanes)] * k,
        flops=4 * s.rows * s.V * x_depth * s.X,
    )
    ends = swap(ends, "gy", s.ny, s.ky)
    rest = run(
        sides_kernel,
        [weights] + faces + corners,
        [shape(s.gz, s.lanes)] * m + [shape(s.ypack, s.lanes)] * k,
    )
    sides, packs = rest[:m], rest[m:]
    packs = swap(packs, "gy", s.ny, s.ky)
    partial = run(
        partial_kernel,
        [w_now, own],
        [jax.ShapeDtypeStruct((s.rows, s.lanes), F32)],
        flops=4 * s.rows * s.rows * s.lanes,
    )[0]
    kernel_rows = top_kernel.reshape(s.top, top_kernel.shape[3])
    started = jnp.zeros((s.top, s.V), F32)
    if doubling(s.ny):
        started = run(
            top_own_kernel, [known, kernel_rows], [jax.ShapeDtypeStruct((s.top, s.V), F32)]
        )[0]
    known = gather(known[None], "gy", s.ny, stack)
    return run(
        final_kernel,
        [partial, w_later] + ends + sides + packs + [started, known, kernel_rows],
        [shape(*field.shape)],
        scratch=buffers,
        far_out=True,
    )[0]


def solution(mesh):
    sizes = tuple(mesh.shape[name] for name in ("gx", "gy", "gz"))

    def body(*args):
        return shards(sizes, *args)

    return jax.shard_map(
        body,
        mesh=mesh,
        in_specs=(P(None, "gz", "gy", "gx"), P(), P(), P("gz", "gy", "gx", None)),
        out_specs=P(None, "gz", "gy", "gx"),
        check_vma=False,
    )
```
